512 devices in a mesh: seq: 32 (over z_hi, x, core), sub: 16 (over z_lo, y).
Axes of the slice: x: 4, y: 4, z: 16 (z_hi: 4, z_lo: 4; z = z_hi * 4 + z_lo), core: 2. Of those that a mesh axis runs over, the one named last changes fastest.
Arguments:
- activations: bfloat16 [65536, 1024], P(('seq', 'sub')), may hold values from -6 to 6
- conv_weight: bfloat16 [5, 1152, 1024], P(None, 'sub'), may hold values from -1 to 1
- cotangent: bfloat16 [16384, 1152], P('seq', 'sub'), may hold values from -6 to 6
Outputs:
- features: bfloat16 [16384, 1152], P('seq', 'sub')
- input_grad: bfloat16 [65536, 1024], P(('seq', 'sub'))
- weight_grad: float32 [1024, 5, 1152], P('seq', None, 'sub')
The draws below stay inside these ranges and needn't reach their ends.
All inputs are finite; a program needn't handle non-finite values.
Results may differ from the reference program's by a relative error of at most 0.02.
Values may be sent and summed in bfloat16 or wider, within the bound.
No kernel may reach another device: no remote copies, remote signals or barrier semaphores. Data moves between devices by JAX's collectives and lax.ppermute only.
A program may use at most 64 MiB of HBM per device.

```python
import math
import jax
import jax.numpy as jnp
from jax import lax

C1 = 1024
C2 = 1152
KW = 5
L1 = 65536
L3 = 16384
N_SUB = 16


def draw_conv_weight(key, part):
    standard_key, roughness_key = jax.random.split(key)
    standard = jax.random.normal(standard_key, (KW, C2, C1), jnp.float32)
    column = jnp.arange(C2).astype(jnp.float32)
    rising = 0.6 + 1.2 * column / C2
    roughness = jnp.exp(jax.random.uniform(roughness_key, (C2,), jnp.float32, -0.35, 0.35))
    scales = (rising * roughness)[None, :, None]
    scaled = standard * scales / math.sqrt(KW * C1)
    return jnp.clip(scaled, -1.0, 1.0).astype(jnp.bfloat16)


def level_of(rng, extent, pieces, least, high):
    gain = 1.0
    for dim, blocks in pieces:
        draws = jax.random.uniform(jax.random.fold_in(jax.random.fold_in(rng, 6), dim), (blocks,), jnp.float32, least / len(pieces), high / len(pieces))
        gain = gain * jnp.repeat(jnp.exp(draws), extent[dim] // blocks).reshape((-1,) + (1,) * (len(extent) - 1 - dim))
    return gain


def scatter_about(stream_key, dims, scale, limit, cuts=(), kind=jnp.bfloat16):
    array = scale * jax.random.normal(stream_key, dims, jnp.float32)
    if cuts:
        array = array * level_of(stream_key, dims, cuts, -0.22, 0.18)
    return jnp.clip(array, -limit, limit).astype(kind)


def setup_inputs(seed: int = 0) -> dict:
    key_list = jax.random.split(jax.random.key(seed), 4)
    return {
        "activations": scatter_about(key_list[0], (L1, C1), 1.0, 6.0, ((0, 512),)),
        "conv_weight": draw_conv_weight(jax.random.fold_in(key_list[3], 71), 0),
        "cotangent": scatter_about(key_list[2], (L3, C2), 1.0, 6.0, ((0, 32), (1, 16))),
    }


EPSILON = 1e-06

def gelu_slope(tensor):
    return 0.5 * (1.0 + jax.scipy.special.erf(tensor * 0.7071067811865476)) + tensor * jnp.exp(-0.5 * tensor * tensor) * 0.3989422804014327

def pool_pairs(tensor):
    half_rows = tensor.shape[0] // 2
    return 0.5 * lax.optimization_barrier(jnp.sum(tensor.reshape(half_rows, 2, tensor.shape[1]), axis=1))

def reference(activations, conv_weight, cotangent):
    tap_count = conv_weight.shape[0]
    x_float = activations.astype(jnp.float32)
    inv_first = lax.rsqrt(lax.optimization_barrier(jnp.mean(x_float * x_float, axis=1, keepdims=True)) + EPSILON)
    normed_first = x_float * inv_first
    pooled = pool_pairs(jax.nn.gelu(normed_first, approximate=False)).astype(jnp.bfloat16)
    seq_half = pooled.shape[0]
    padded = jnp.pad(pooled, ((2, 2), (0, 0)))
    conv_acc = jnp.zeros((seq_half, C2), jnp.float32)
    for offset in range(tap_count):
        conv_acc = conv_acc + lax.dot_general(padded[offset:offset + seq_half], conv_weight[offset], (((1,), (1,)), ((), ())), preferred_element_type=jnp.float32)
    conv_out = conv_acc.astype(jnp.bfloat16)
    y_float = conv_out.astype(jnp.float32)
    inv_second = lax.rsqrt(lax.optimization_barrier(jnp.mean(y_float * y_float, axis=1, keepdims=True)) + EPSILON)
    normed_second = y_float * inv_second
    features = pool_pairs(jax.nn.gelu(normed_second, approximate=False)).astype(jnp.bfloat16)
    upstream = 0.5 * jnp.repeat(cotangent.astype(jnp.float32), 2, axis=0)
    slope_second = upstream * gelu_slope(normed_second)
    inner_second = lax.optimization_barrier(jnp.mean(slope_second * normed_second, axis=1, keepdims=True))
    conv_grad = (inv_second * (slope_second - normed_second * inner_second)).astype(jnp.bfloat16)
    grad_padded = jnp.pad(conv_grad, ((2, 2), (0, 0)))
    group_width = C2 // N_SUB
    pooled_grad = jnp.zeros((seq_half, C1), jnp.float32)
    for group in range(N_SUB):
        lower_col = group * group_width
        upper_col = lower_col + group_width
        partial_sum = jnp.zeros((seq_half, C1), jnp.float32)
        for offset in range(tap_count):
            partial_sum = partial_sum + jnp.dot(grad_padded[4 - offset:4 - offset + seq_half, lower_col:upper_col], conv_weight[offset, lower_col:upper_col, :], preferred_element_type=jnp.float32)
        rounded = lax.optimization_barrier(partial_sum.astype(jnp.bfloat16))
        pooled_grad = pooled_grad + rounded.astype(jnp.float32)
    slope_first = 0.5 * jnp.repeat(pooled_grad, 2, axis=0) * gelu_slope(normed_first)
    inner_first = lax.optimization_barrier(jnp.mean(slope_first * normed_first, axis=1, keepdims=True))
    input_grad = (inv_first * (slope_first - normed_first * inner_first)).astype(jnp.bfloat16)
    weight_parts = [jnp.dot(padded[offset:offset + seq_half].T, conv_grad, preferred_element_type=jnp.float32) for offset in range(tap_count)]
    weight_grad = jnp.stack(weight_parts, axis=1)
    return (features, input_grad, weight_grad)
```

```python
import jax
import jax.numpy as jnp
from jax import lax
from jax.sharding import Mesh, PartitionSpec as P

EPSILON = 1e-06
AXES = ("zh", "x", "core", "zl", "y")
SEQ = ("zh", "x", "core")
SUB = ("zl", "y")
bf16 = jnp.bfloat16
f32 = jnp.float32


def gelu_slope(tensor):
    return (
        0.5 * (1.0 + jax.scipy.special.erf(tensor * 0.7071067811865476))
        + tensor * jnp.exp(-0.5 * tensor * tensor) * 0.3989422804014327
    )


def pool_pairs(tensor):
    half_rows = tensor.shape[0] // 2
    return 0.5 * jnp.sum(tensor.reshape(half_rows, 2, tensor.shape[1]), axis=1)


def shift(block, axis, step):
    count = lax.axis_size(axis)
    pairs = [(i, i + step) for i in range(count) if 0 <= i + step < count]
    return lax.ppermute(block, axis, pairs)


def padded_2(block):
    low = shift(block[-2:], SEQ, 1)
    high = shift(block[:2], SEQ, -1)
    return jnp.concatenate([low, block, high], axis=0)


def gather_all(block, axis):
    count = lax.axis_size(axis)
    return lax.all_to_all(jnp.broadcast_to(block, (count, *block.shape)), axis, 0, 0)


def small_sum(vector):
    return jnp.sum(gather_all(vector.reshape(8, 128), SUB), axis=0).reshape(-1)


def per_device(activations, conv_weight, cotangent):
    tap_count, out_width, in_width = conv_weight.shape
    full_out = out_width * lax.axis_size(SUB)
    x_float = activations.astype(f32)
    inv_first = lax.rsqrt(jnp.mean(x_float * x_float, axis=1, keepdims=True) + EPSILON)
    normed_first = x_float * inv_first
    pooled = pool_pairs(jax.nn.gelu(normed_first, approximate=False)).astype(bf16)
    gathered = gather_all(pooled, SUB).reshape(-1, in_width)
    rows = gathered.shape[0]
    padded = padded_2(gathered)
    conv_acc = jnp.zeros((rows, out_width), f32)
    for k in range(tap_count):
        conv_acc = conv_acc + lax.dot_general(
            padded[k : k + rows], conv_weight[k], (((1,), (1,)), ((), ())),
            preferred_element_type=f32,
        )
    conv_out = conv_acc.astype(bf16)
    y_float = conv_out.astype(f32)
    square_sum = small_sum(jnp.sum(y_float * y_float, axis=1))
    inv_second = lax.rsqrt(square_sum / full_out + EPSILON)[:, None]
    normed_second = y_float * inv_second
    features = pool_pairs(jax.nn.gelu(normed_second, approximate=False)).astype(bf16)
    upstream = 0.5 * jnp.repeat(cotangent.astype(f32), 2, axis=0)
    slope_second = upstream * gelu_slope(normed_second)
    inner_second = small_sum(jnp.sum(slope_second * normed_second, axis=1))
    conv_grad = (
        inv_second * (slope_second - normed_second * (inner_second / full_out)[:, None])
    ).astype(bf16)
    grad_padded = padded_2(conv_grad)
    windows = [grad_padded[4 - k : 4 - k + rows] for k in range(tap_count)]
    running = jnp.zeros((rows, in_width), f32)
    for k in range(tap_count):
        running = running + jnp.dot(windows[k], conv_weight[k], preferred_element_type=f32)
    parts = lax.all_to_all(running.astype(bf16).reshape(16, -1, in_width), SUB, 0, 0)
    pooled_grad = jnp.sum(parts.astype(f32), axis=0)
    slope_first = 0.5 * jnp.repeat(pooled_grad, 2, axis=0) * gelu_slope(normed_first)
    inner_first = jnp.mean(slope_first * normed_first, axis=1, keepdims=True)
    input_grad = (inv_first * (slope_first - normed_first * inner_first)).astype(bf16)

    wide = jnp.concatenate(windows, axis=1)
    weight_part = lax.dot_general(
        gathered, wide, (((0,), (0,)), ((), ())), preferred_element_type=f32
    )
    core = lax.axis_index("core")
    halves = weight_part.reshape(16, 2, 32, tap_count * out_width)
    mine = jnp.where(core == 0, halves[:, 0], halves[:, 1])
    other = jnp.where(core == 0, halves[:, 1], halves[:, 0]).astype(bf16)
    total = mine + lax.ppermute(other, "core", [(0, 1), (1, 0)]).astype(f32)
    total = total.reshape(4, 4, 32, -1).transpose(1, 0, 2, 3).astype(bf16)
    total = jnp.sum(lax.all_to_all(total, "x", 0, 0).astype(f32), axis=0)
    total = jnp.sum(lax.all_to_all(total.astype(bf16), "zh", 0, 0).astype(f32), axis=0)
    weight_grad = total.reshape(32, tap_count, out_width)
    return (features, input_grad, weight_grad)


def solution(mesh):
    split = Mesh(mesh.devices.reshape(4, 4, 2, 4, 4), AXES)
    return jax.shard_map(
        per_device,
        mesh=split,
        in_specs=(P(AXES, None), P(None, SUB, None), P(SEQ, SUB)),
        out_specs=(P(SEQ, SUB), P(AXES, None), P(SEQ, None, SUB)),
        check_vma=False,
    )
```

```python
import jax
import jax.numpy as jnp
from jax import lax
from jax.sharding import Mesh, PartitionSpec as P

EPSILON = 1e-06
AXES = ("zh", "x", "core", "zl", "y")
SEQ = ("zh", "x", "core")
SUB = ("zl", "y")
bf16 = jnp.bfloat16
f32 = jnp.float32


def gelu_slope(tensor):
    return (
        0.5 * (1.0 + jax.scipy.special.erf(tensor * 0.7071067811865476))
        + tensor * jnp.exp(-0.5 * tensor * tensor) * 0.3989422804014327
    )


def pool_pairs(tensor):
    half_rows = tensor.shape[0] // 2
    return 0.5 * jnp.sum(tensor.reshape(half_rows, 2, tensor.shape[1]), axis=1)


def shift(block, axis, step):
    count = lax.axis_size(axis)
    pairs = [(i, i + step) for i in range(count) if 0 <= i + step < count]
    return lax.ppermute(block, axis, pairs)


def gather_all(block, axis):
    count = lax.axis_size(axis)
    return lax.all_to_all(jnp.broadcast_to(block, (count, *block.shape)), axis, 0, 0)


def rms_normed(rows):
    wide = rows.astype(f32)
    inv = lax.rsqrt(jnp.mean(wide * wide, axis=1, keepdims=True) + EPSILON)
    return wide * inv, inv


def pooled_of(normed):
    return pool_pairs(jax.nn.gelu(normed, approximate=False)).astype(bf16)


def per_device(activations, conv_weight, cotangent):
    tap_count, out_width, in_width = conv_weight.shape
    full_out = out_width * lax.axis_size(SUB)
    core = lax.axis_index("core")
    half = in_width // 2
    rows = activations.shape[0] // 2
    span = rows + 8
    group = 4 * out_width

    own_half = jnp.where(core == 0, conv_weight[:, :, :half], conv_weight[:, :, half:])
    first = gather_all(own_half, "y")
    second = lax.ppermute(first, "core", [(0, 1), (1, 0)])
    weights = jnp.where(
        core == 0,
        jnp.concatenate([first, second], axis=3),
        jnp.concatenate([second, first], axis=3),
    )
    weights = weights.transpose(1, 0, 2, 3).reshape(tap_count, group, in_width)

    low = shift(activations[-8:], AXES, 1)
    high = shift(activations[:8], AXES, -1)
    normed_first, inv_first = rms_normed(activations)
    pooled = pooled_of(normed_first)
    edges = pooled_of(rms_normed(jnp.concatenate([low, high], axis=0))[0])
    block = jnp.concatenate([edges[:4], pooled, edges[4:]], axis=0)
    gathered = gather_all(block, "zl")
    flat = jnp.concatenate(
        [gathered.reshape(4 * span, in_width), jnp.zeros((4, in_width), bf16)], axis=0
    )
    around = gather_all(gathered[:, 4 : 4 + rows].reshape(4 * rows, in_width), "y")

    cot = cotangent.T
    pairs = span // 2
    before = shift(cot[:, -1:], SEQ, 1)
    after = shift(cot[:, :1], SEQ, -1)
    place = jnp.arange(4)[:, None, None] + 4 * jnp.arange(4)[None, :, None]
    source = place * (rows // 2) + jnp.arange(pairs)[None, None, :] - 1
    source = jnp.where(jnp.arange(pairs)[None, None, :] < pairs - 2, source, -2)
    source = source.reshape(4, 1, 4 * pairs)
    pick = (source == jnp.arange(cot.shape[1])[None, :, None]).astype(bf16)
    spread = jnp.einsum("or,yrz->yoz", cot, pick, preferred_element_type=f32)
    spread = (
        spread
        + jnp.where(source == -1, before.astype(f32)[None], 0.0)
        + jnp.where(source == cot.shape[1], after.astype(f32)[None], 0.0)
    ).astype(bf16)
    cot_block = lax.all_to_all(spread, "y", 0, 0).reshape(group, 4 * pairs)
    lanes = 4 * span
    repeat = (jnp.arange(4 * pairs)[:, None] == jnp.arange(lanes)[None, :] // 2).astype(bf16)
    upstream = 0.5 * jnp.dot(cot_block, repeat, preferred_element_type=f32)

    conv_acc = jnp.zeros((group, lanes), f32)
    for k in range(tap_count):
        conv_acc = conv_acc + lax.dot_general(
            weights[k], flat[k : k + lanes], (((1,), (1,)), ((), ())),
            preferred_element_type=f32,
        )
    y_float = conv_acc.astype(bf16).astype(f32)
    square_sum = lax.psum(jnp.sum(y_float * y_float, axis=0), "zl")
    inv_second = lax.rsqrt(square_sum / full_out + EPSILON)[None, :]
    normed_second = y_float * inv_second
    slope_second = upstream * gelu_slope(normed_second)
    inner_second = lax.psum(jnp.sum(slope_second * normed_second, axis=0), "zl")
    conv_grad = inv_second * (slope_second - normed_second * (inner_second / full_out)[None, :])
    inside = (jnp.arange(lanes) % span < rows + 4)[None, :]
    conv_grad = jnp.where(inside, conv_grad, 0.0).astype(bf16)
    active = jax.nn.gelu(normed_second, approximate=False)
    features = 0.5 * lax.dot_general(
        active, repeat.astype(f32), (((1,), (1,)), ((), ())),
        precision=lax.Precision.HIGHEST, preferred_element_type=f32,
    )

    sent = jnp.concatenate([conv_grad, features.astype(bf16)], axis=1)
    back = lax.all_to_all(sent.reshape(4, out_width, -1), "y", 0, 0)
    feature_back = back[:, :, lanes:].reshape(4, out_width, 4, pairs)[..., 1 : 1 + rows // 2]
    features = feature_back.transpose(2, 0, 3, 1).reshape(-1, out_width)
    grad_back = back[:, :, :lanes].reshape(4, out_width, 4, span)

    grad_flat = jnp.concatenate([conv_grad, jnp.zeros((group, 4), bf16)], axis=1)
    running = jnp.zeros((lanes, in_width), f32)
    for k in range(tap_count):
        running = running + lax.dot_general(
            grad_flat[:, 4 - k : 4 - k + lanes], weights[k], (((0,), (0,)), ((), ())),
            preferred_element_type=f32,
        )
    running = running.astype(bf16).reshape(4, span, in_width)[:, :rows]
    parts = lax.all_to_all(running, "zl", 0, 0)
    pooled_grad = jnp.sum(parts.astype(f32), axis=0)
    slope_first = 0.5 * jnp.repeat(pooled_grad, 2, axis=0) * gelu_slope(normed_first)
    inner_first = jnp.mean(slope_first * normed_first, axis=1, keepdims=True)
    input_grad = (inv_first * (slope_first - normed_first * inner_first)).astype(bf16)

    windows = jnp.stack([grad_back[..., 4 - k : 4 - k + rows] for k in range(tap_count)])
    wide = windows.transpose(0, 2, 1, 3, 4).reshape(tap_count * out_width, -1)
    weight_part = lax.dot_general(
        around.reshape(-1, in_width), wide, (((0,), (1,)), ((), ())),
        preferred_element_type=f32,
    )
    halves = weight_part.reshape(16, 2, in_width // 32, tap_count * out_width)
    mine = jnp.where(core == 0, halves[:, 0], halves[:, 1])
    other = jnp.where(core == 0, halves[:, 1], halves[:, 0]).astype(bf16)
    total = mine + lax.ppermute(other, "core", [(0, 1), (1, 0)]).astype(f32)
    total = lax.all_to_all(total.astype(bf16), ("zh", "x"), 0, 0)
    weight_grad = jnp.sum(total.astype(f32), axis=0).reshape(-1, tap_count, out_width)
    return (features, input_grad, weight_grad)


def solution(mesh):
    split = Mesh(mesh.devices.reshape(4, 4, 2, 4, 4), AXES)
    return jax.shard_map(
        per_device,
        mesh=split,
        in_specs=(P(AXES, None), P(None, SUB, None), P(SEQ, SUB)),
        out_specs=(P(SEQ, SUB), P(AXES, None), P(SEQ, None, SUB)),
        check_vma=False,
    )
```

```python
import functools

import jax
import jax.numpy as jnp
from jax import lax
from jax.experimental import pallas as pl
from jax.experimental.pallas import tpu as pltpu
from jax.sharding import Mesh, PartitionSpec as P


EPSILON = 1e-06
AXES = ("zh", "x", "core", "zl", "y")
SEQ = ("zh", "x", "core")
SUB = ("zl", "y")
bf16 = jnp.bfloat16
f32 = jnp.float32


def half_erf(tensor):
    return 0.5 * (1.0 + lax.erf(tensor * 0.7071067811865476))


def gelu_slope(tensor, half):
    return half + tensor * jnp.exp(-0.5 * tensor * tensor) * 0.3989422804014327


def shift(block, axis, step):
    count = lax.axis_size(axis)
    pairs = [(i, i + step) for i in range(count) if 0 <= i + step < count]
    return lax.ppermute(block, axis, pairs)


def turn(block, axis, step):
    count = lax.axis_size(axis)
    return lax.ppermute(block, axis, [(i, (i + step) % count) for i in range(count)])


def gather_all(block, axis):
    count = lax.axis_size(axis)
    return lax.all_to_all(jnp.broadcast_to(block, (count, *block.shape)), axis, 0, 0)


def local_call(kernel, shapes, scratch, *args):
    vmem = pl.BlockSpec(memory_space=pltpu.VMEM)
    return pl.pallas_call(
        kernel,
        out_shape=shapes,
        in_specs=[vmem] * len(args),
        out_specs=jax.tree.map(lambda _: vmem, shapes),
        scratch_shapes=scratch,
        compiler_params=pltpu.CompilerParams(vmem_limit_bytes=12 << 20),
    )(*args)


def exact_dot(left, right):
    return jnp.dot(left, right, precision=lax.Precision.HIGHEST, preferred_element_type=f32)


def pair_mean(count, rows, first):
    pair = lax.broadcasted_iota(jnp.int32, (count, rows), 0)
    row = lax.broadcasted_iota(jnp.int32, (count, rows), 1)
    return jnp.where((row - first >= 2 * pair) & (row - first <= 2 * pair + 1), 0.5, 0.0)


def pooled_kernel(low_ref, own_ref, high_ref, out_ref, gelu_ref):
    at = 0
    for ref in (low_ref, own_ref, high_ref):
        count = ref.shape[0]
        wide = ref[...].astype(f32)
        inv = lax.rsqrt(jnp.mean(wide * wide, axis=1, keepdims=True) + EPSILON)
        normed = wide * inv
        gelu_ref[at : at + count, :] = normed * half_erf(normed)
        at += count
    out_ref[...] = exact_dot(pair_mean(at // 2, at, 0), gelu_ref[...]).astype(bf16)


def pooled_block(low, own, high):
    total = low.shape[0] + own.shape[0] + high.shape[0]
    width = own.shape[1]
    return local_call(
        pooled_kernel, jax.ShapeDtypeStruct((total // 2, width), bf16),
        [pltpu.VMEM((total, width), f32)], low, own, high,
    )


def windows_kernel(before_ref, cot_ref, after_ref, out_ref, wide_ref):
    count, rows, _ = out_ref.shape
    step = (cot_ref.shape[0]) // count
    wide_ref[...] = jnp.zeros_like(wide_ref)
    wide_ref[7:8, :] = before_ref[...].astype(f32)
    wide_ref[8 : 8 + cot_ref.shape[0], :] = cot_ref[...].astype(f32)
    wide_ref[8 + cot_ref.shape[0] : 9 + cot_ref.shape[0], :] = after_ref[...].astype(f32)
    for b in range(count):
        out_ref[b] = wide_ref[pl.ds(7 + step * b, rows), :].astype(bf16)


def cot_windows(before, cot, after, count):
    rows, width = cot.shape
    return local_call(
        windows_kernel,
        jax.ShapeDtypeStruct((count, rows // count + 8, width), bf16),
        [pltpu.VMEM((rows + 24, width), f32)], before, cot, after,
    )


def statistics_kernel(own, y_ref, cot_ref, grad_ref, back_ref):
    groups, rows, width = y_ref.shape
    full = groups * width
    pairs = cot_ref.shape[1]
    block = width // 4
    repeat = (
        lax.broadcasted_iota(jnp.int32, (rows, pairs), 0) // 2
        == lax.broadcasted_iota(jnp.int32, (rows, pairs), 1)
    ).astype(bf16)
    source = lax.broadcasted_iota(jnp.int32, (width, 512), 0)
    lane = lax.broadcasted_iota(jnp.int32, (width, 512), 1)
    spread = ((lane % 128 < block) & (source == lane // 128 * block + lane % 128)).astype(bf16)
    means = pair_mean(own // 2, rows, 2)
    keep = (
        lax.broadcasted_iota(jnp.int32, (own, rows), 0) + 2
        == lax.broadcasted_iota(jnp.int32, (own, rows), 1)
    ).astype(bf16)
    square = 0.0
    for g in range(groups):
        wide = y_ref[g].astype(f32)
        square = square + jnp.sum(wide * wide, axis=1, keepdims=True)
    inv = lax.rsqrt(square / full + EPSILON)
    slopes, inner = [], 0.0
    for g in range(groups):
        normed = y_ref[g].astype(f32) * inv
        half = half_erf(normed)
        features = exact_dot(means, normed * half).astype(bf16)
        placed = jnp.dot(features, spread, preferred_element_type=f32).astype(bf16)
        for i in range(4):
            back_ref[4 * g + i, : own // 2, :] = placed[:, 128 * i : 128 * i + 128]
        upstream = 0.5 * jnp.dot(repeat, cot_ref[g], preferred_element_type=f32)
        slope = upstream * gelu_slope(normed, half)
        inner = inner + jnp.sum(slope * normed, axis=1, keepdims=True)
        slopes.append(slope)
    mean = inner / full
    for g in range(groups):
        normed = y_ref[g].astype(f32) * inv
        grad = (inv * (slopes[g] - normed * mean)).astype(bf16)
        grad_ref[g] = grad
        mine = jnp.dot(keep, grad, preferred_element_type=f32).astype(bf16)
        placed = jnp.dot(mine, spread, preferred_element_type=f32).astype(bf16)
        for i in range(4):
            back_ref[4 * g + i, own // 2 :, :] = placed[:, 128 * i : 128 * i + 128]


def statistics(conv_out, cot, own):
    groups = conv_out.shape[0]
    shapes = (
        jax.ShapeDtypeStruct(conv_out.shape, bf16),
        jax.ShapeDtypeStruct((4 * groups, own + own // 2, 128), bf16),
    )
    kernel = functools.partial(statistics_kernel, own)
    return local_call(kernel, shapes, [], conv_out, cot)


def taps_kernel(taps, back_ref, wide_ref, feature_ref, stage_ref):
    count, rows, lanes = back_ref.shape
    own = 2 * rows // 3
    span = stage_ref.shape[0] // count
    width = wide_ref.shape[1]
    block = width // taps
    source = lax.broadcasted_iota(jnp.int32, (lanes, width), 0)
    lane = lax.broadcasted_iota(jnp.int32, (lanes, width), 1)
    total = jnp.zeros((count * span, width), f32)
    for k in range(taps):
        stage_ref[...] = jnp.zeros_like(stage_ref)
        for b in range(count):
            stage_ref[pl.ds(b * span + k + 2, own), :] = back_ref[b, own // 2 :, :].astype(f32)
        place = ((source < block) & (lane == source + k * block)).astype(bf16)
        total = total + jnp.dot(stage_ref[...].astype(bf16), place, preferred_element_type=f32)
    wide_ref[...] = total.astype(bf16)
    for b in range(count):
        feature_ref[pl.ds(b * (own // 2), own // 2), :] = back_ref[b, : own // 2, :block]


def spread_taps(back, taps, block, span):
    count, rows, lanes = back.shape
    shapes = (
        jax.ShapeDtypeStruct((count * span, taps * block), bf16),
        jax.ShapeDtypeStruct((count * (rows // 3), block), bf16),
    )
    kernel = functools.partial(taps_kernel, taps)
    return local_call(kernel, shapes, [pltpu.VMEM((count * span, lanes), f32)], back)


def per_device(activations, conv_weight, cotangent):
    tap_count, out_width, in_width = conv_weight.shape
    core = lax.axis_index("core")
    zl, y = lax.axis_index("zl"), lax.axis_index("y")
    half = in_width // 2
    rows = activations.shape[0] // 2
    span = rows + 8
    group = 4 * out_width
    lanes = 4 * span

    low = shift(activations[-8:], AXES, 1)
    high = shift(activations[:8], AXES, -1)

    own_half = jnp.where(core == 0, conv_weight[:, :, :half], conv_weight[:, :, half:])
    first = gather_all(own_half, "y")
    second = lax.ppermute(first, "core", [(0, 1), (1, 0)])
    weights = jnp.where(
        core == 0,
        jnp.concatenate([first, second], axis=3),
        jnp.concatenate([second, first], axis=3),
    )
    weights = weights.transpose(1, 0, 2, 3).reshape(tap_count, group, in_width)

    block = pooled_block(low, activations, high)
    blocks = [block] + [turn(block, "zl", j) for j in (1, 2, 3)]
    gathered = jnp.zeros((5, span, in_width), bf16)
    for j in range(4):
        gathered = lax.dynamic_update_index_in_dim(gathered, blocks[j], (zl - j) % 4, 0)
    flat = gathered.reshape(-1, in_width)

    cot, _ = lax.optimization_barrier((cotangent, block))
    before = shift(cot[-1:], SEQ, 1)
    after = shift(cot[:1], SEQ, -1)
    step = rows // 2
    windows = cot_windows(before, cot, after, 16)
    windows = lax.all_to_all(windows, SUB, 0, 0)
    cot_block = windows.reshape(4, 4, step + 8, out_width).transpose(0, 2, 1, 3)
    cot_block = cot_block.reshape(4, step + 8, group)

    conv_acc = jnp.zeros((lanes, group), f32)
    for k in range(tap_count):
        conv_acc = conv_acc + lax.dot_general(
            flat[k : k + lanes], weights[k], (((1,), (1,)), ((), ())),
            preferred_element_type=f32,
        )
    conv_out = conv_acc.astype(bf16).reshape(4, span, group)
    near = gathered[:4].reshape(lanes, in_width)
    ring = [near] + [turn(near, "y", j) for j in (1, 2, 3)]
    conv_out = lax.all_to_all(conv_out, "zl", 0, 0)
    grad, back = statistics(conv_out, cot_block, rows)
    back = lax.all_to_all(back, SUB, 0, 0)
    grad = lax.all_to_all(grad, "zl", 0, 0)

    grad_flat = jnp.concatenate([grad.reshape(lanes, group), jnp.zeros((8, group), bf16)], axis=0)
    running = jnp.zeros((lanes, in_width), f32)
    for k in range(tap_count):
        running = running + jnp.dot(
            grad_flat[4 - k : 4 - k + lanes], weights[k], preferred_element_type=f32
        )
    running = running.astype(bf16).reshape(4, span, in_width)
    own = [
        lax.dynamic_slice(running, ((zl + j) % 4, 0, 0), (1, rows, in_width))[0]
        for j in range(4)
    ]
    parts = own[:1] + [turn(own[j], "zl", j) for j in (1, 2, 3)]
    pooled_grad = sum(part.astype(f32) for part in parts)
    x_float = activations.astype(f32)
    inv_first = lax.rsqrt(jnp.mean(x_float * x_float, axis=1, keepdims=True) + EPSILON)
    normed_first = x_float * inv_first
    slope_first = 0.5 * jnp.repeat(pooled_grad, 2, axis=0)
    slope_first = slope_first * gelu_slope(normed_first, half_erf(normed_first))
    inner_first = jnp.mean(slope_first * normed_first, axis=1, keepdims=True)
    input_grad = (inv_first * (slope_first - normed_first * inner_first)).astype(bf16)

    around = jnp.zeros((4, 4, span, in_width), bf16)
    for j in range(4):
        piece = ring[j].reshape(4, 1, span, in_width)
        around = lax.dynamic_update_slice_in_dim(around, piece, (y - j) % 4, axis=1)
    wide, features = spread_taps(back, tap_count, out_width, span)
    weight_part = lax.dot_general(
        around.reshape(-1, in_width), wide, (((0,), (0,)), ((), ())),
        preferred_element_type=f32,
    )
    halves = weight_part.reshape(16, 2, in_width // 32, tap_count * out_width)
    mine = jnp.where(core == 0, halves[:, 0], halves[:, 1])
    other = jnp.where(core == 0, halves[:, 1], halves[:, 0]).astype(bf16)
    other = lax.ppermute(other, "core", [(0, 1), (1, 0)])
    total = (mine + other.astype(f32)).astype(bf16)
    total = lax.all_to_all(total, ("zh", "x"), 0, 0)
    weight_grad = jnp.sum(total.astype(f32), axis=0).reshape(-1, tap_count, out_width)
    return (features, input_grad, weight_grad)


def solution(mesh):
    split = Mesh(mesh.devices.reshape(4, 4, 2, 4, 4), AXES)
    return jax.shard_map(
        per_device,
        mesh=split,
        in_specs=(P(AXES, None), P(None, SUB, None), P(SEQ, SUB)),
        out_specs=(P(SEQ, SUB), P(AXES, None), P(SEQ, None, SUB)),
        check_vma=False,
    )
```

```python
import functools

import jax
import jax.numpy as jnp
from jax import lax
from jax.experimental import pallas as pl
from jax.experimental.pallas import tpu as pltpu
from jax.sharding import Mesh, PartitionSpec as P


EPSILON = 1e-06
AXES = ("zh", "x", "core", "zl", "y")
SEQ = ("zh", "x", "core")
SUB = ("zl", "y")
bf16 = jnp.bfloat16
f32 = jnp.float32


def half_erf(tensor):
    return 0.5 * (1.0 + lax.erf(tensor * 0.7071067811865476))


def gelu_slope(tensor, half):
    return half + tensor * jnp.exp(-0.5 * tensor * tensor) * 0.3989422804014327


def shift(block, axis, step):
    count = lax.axis_size(axis)
    pairs = [(i, i + step) for i in range(count) if 0 <= i + step < count]
    return lax.ppermute(block, axis, pairs)


def turn(block, axis, step):
    count = lax.axis_size(axis)
    return lax.ppermute(block, axis, [(i, (i + step) % count) for i in range(count)])


def gather_all(block, axis):
    count = lax.axis_size(axis)
    return lax.all_to_all(jnp.broadcast_to(block, (count, *block.shape)), axis, 0, 0)


def local_call(kernel, shapes, scratch, *args):
    vmem = pl.BlockSpec(memory_space=pltpu.VMEM)
    return pl.pallas_call(
        kernel,
        out_shape=shapes,
        in_specs=[vmem] * len(args),
        out_specs=jax.tree.map(lambda _: vmem, shapes),
        scratch_shapes=scratch,
        compiler_params=pltpu.CompilerParams(vmem_limit_bytes=12 << 20),
    )(*args)


def exact_dot(left, right):
    return jnp.dot(left, right, precision=lax.Precision.HIGHEST, preferred_element_type=f32)


def pair_mean(count, rows, first):
    pair = lax.broadcasted_iota(jnp.int32, (count, rows), 0)
    row = lax.broadcasted_iota(jnp.int32, (count, rows), 1)
    return jnp.where((row - first >= 2 * pair) & (row - first <= 2 * pair + 1), 0.5, 0.0)


def pooled_kernel(low_ref, own_ref, high_ref, out_ref, gelu_ref):
    at = 0
    for ref in (low_ref, own_ref, high_ref):
        count = ref.shape[0]
        wide = ref[...].astype(f32)
        inv = lax.rsqrt(jnp.mean(wide * wide, axis=1, keepdims=True) + EPSILON)
        normed = wide * inv
        gelu_ref[at : at + count, :] = normed * half_erf(normed)
        at += count
    out_ref[...] = exact_dot(pair_mean(at // 2, at, 0), gelu_ref[...]).astype(bf16)


def pooled_block(low, own, high):
    total = low.shape[0] + own.shape[0] + high.shape[0]
    width = own.shape[1]
    return local_call(
        pooled_kernel, jax.ShapeDtypeStruct((total // 2, width), bf16),
        [pltpu.VMEM((total, width), f32)], low, own, high,
    )


def windows_kernel(before_ref, cot_ref, after_ref, out_ref, wide_ref):
    count, rows, _ = out_ref.shape
    step = (cot_ref.shape[0]) // count
    wide_ref[...] = jnp.zeros_like(wide_ref)
    wide_ref[7:8, :] = before_ref[...].astype(f32)
    wide_ref[8 : 8 + cot_ref.shape[0], :] = cot_ref[...].astype(f32)
    wide_ref[8 + cot_ref.shape[0] : 9 + cot_ref.shape[0], :] = after_ref[...].astype(f32)
    for b in range(count):
        out_ref[b] = wide_ref[pl.ds(7 + step * b, rows), :].astype(bf16)


def cot_windows(before, cot, after, count):
    rows, width = cot.shape
    return local_call(
        windows_kernel,
        jax.ShapeDtypeStruct((count, rows // count + 8, width), bf16),
        [pltpu.VMEM((rows + 24, width), f32)], before, cot, after,
    )


def statistics_kernel(own, y_ref, cot_ref, grad_ref, back_ref):
    groups, rows, width = y_ref.shape
    full = groups * width
    pairs = cot_ref.shape[1]
    block = width // 4
    repeat = (
        lax.broadcasted_iota(jnp.int32, (rows, pairs), 0) // 2
        == lax.broadcasted_iota(jnp.int32, (rows, pairs), 1)
    ).astype(bf16)
    source = lax.broadcasted_iota(jnp.int32, (width, 512), 0)
    lane = lax.broadcasted_iota(jnp.int32, (width, 512), 1)
    spread = ((lane % 128 < block) & (source == lane // 128 * block + lane % 128)).astype(bf16)
    means = pair_mean(own // 2, rows, 2)
    square = 0.0
    for g in range(groups):
        wide = y_ref[g].astype(f32)
        square = square + jnp.sum(wide * wide, axis=1, keepdims=True)
    inv = lax.rsqrt(square / full + EPSILON)
    slopes, inner = [], 0.0
    for g in range(groups):
        normed = y_ref[g].astype(f32) * inv
        half = half_erf(normed)
        features = exact_dot(means, normed * half).astype(bf16)
        placed = jnp.dot(features, spread, preferred_element_type=f32).astype(bf16)
        for i in range(4):
            back_ref[4 * g + i, : own // 2, :] = placed[:, 128 * i : 128 * i + 128]
        upstream = 0.5 * jnp.dot(repeat, cot_ref[g], preferred_element_type=f32)
        slope = upstream * gelu_slope(normed, half)
        inner = inner + jnp.sum(slope * normed, axis=1, keepdims=True)
        slopes.append(slope)
    mean = inner / full
    for g in range(groups):
        normed = y_ref[g].astype(f32) * inv
        grad = (inv * (slopes[g] - normed * mean)).astype(bf16)
        grad_ref[g] = grad
        placed = jnp.dot(grad, spread, preferred_element_type=f32).astype(bf16)
        for i in range(4):
            back_ref[4 * g + i, own // 2 :, :] = placed[:, 128 * i : 128 * i + 128]


def statistics(conv_out, cot, own):
    groups = conv_out.shape[0]
    shapes = (
        jax.ShapeDtypeStruct(conv_out.shape, bf16),
        jax.ShapeDtypeStruct((4 * groups, conv_out.shape[1] + own // 2, 128), bf16),
    )
    kernel = functools.partial(statistics_kernel, own)
    return local_call(kernel, shapes, [], conv_out, cot)


def taps_kernel(taps, back_ref, wide_ref, feature_ref, frame_ref, stage_ref):
    count, rows, lanes = back_ref.shape
    span = frame_ref.shape[1]
    pooled = rows - span
    own = 2 * pooled
    width = wide_ref.shape[1]
    block = width // taps
    source = lax.broadcasted_iota(jnp.int32, (lanes, width), 0)
    lane = lax.broadcasted_iota(jnp.int32, (lanes, width), 1)
    for b in range(count):
        frame_ref[b] = back_ref[b, pooled:, :].astype(f32)
        feature_ref[pl.ds(b * pooled, pooled), :] = back_ref[b, :pooled, :block]
    total = jnp.zeros((count * own, width), f32)
    for k in range(taps):
        for b in range(count):
            at = (b % 4 * 4 + b // 4) * own
            stage_ref[pl.ds(at, own), :] = frame_ref[b, pl.ds(4 - k, own), :].astype(bf16)
        place = ((source < block) & (lane == source + k * block)).astype(bf16)
        total = total + jnp.dot(stage_ref[...], place, preferred_element_type=f32)
    wide_ref[...] = total.astype(bf16)


def spread_taps(back, taps, block, own):
    count, rows, lanes = back.shape
    shapes = (
        jax.ShapeDtypeStruct((count * own, taps * block), bf16),
        jax.ShapeDtypeStruct((count * own // 2, block), bf16),
    )
    scratch = [
        pltpu.VMEM((count, rows - own // 2, lanes), f32),
        pltpu.VMEM((count * own, lanes), bf16),
    ]
    return local_call(functools.partial(taps_kernel, taps), shapes, scratch, back)


def per_device(activations, conv_weight, cotangent):
    tap_count, out_width, in_width = conv_weight.shape
    core = lax.axis_index("core")
    zl, y = lax.axis_index("zl"), lax.axis_index("y")
    half = in_width // 2
    rows = activations.shape[0] // 2
    span = rows + 8
    group = 4 * out_width
    lanes = 4 * span
    step = rows // 2

    low = shift(activations[-8:], AXES, 1)
    high = shift(activations[:8], AXES, -1)

    own_half = jnp.where(core == 0, conv_weight[:, :, :half], conv_weight[:, :, half:])
    own_half = lax.optimization_barrier(own_half)
    shards = [own_half] + [turn(own_half, "y", j) for j in (1, 2, 3)]
    first = jnp.zeros((tap_count, 4, out_width, half), bf16)
    first = lax.dynamic_update_slice_in_dim(first, shards[0][:, None], y, axis=1)
    for j in range(1, 4):
        first = lax.dynamic_update_slice_in_dim(first, shards[j][:, None], (y - j) % 4, axis=1)
    first = first.reshape(tap_count, group, half)
    second = lax.ppermute(first, "core", [(0, 1), (1, 0)])

    block = pooled_block(low, activations, high)
    gathered = gather_all(block, "zl")
    flat = jnp.concatenate(
        [gathered.reshape(lanes, in_width), jnp.zeros((8, in_width), bf16)], axis=0
    )
    flat_first = jnp.where(core == 0, flat[:, :half], flat[:, half:])
    flat_second = jnp.where(core == 0, flat[:, half:], flat[:, :half])

    cot, _ = lax.optimization_barrier((cotangent, block))
    before = shift(cot[-1:], SEQ, 1)
    after = shift(cot[:1], SEQ, -1)
    windows = cot_windows(before, cot, after, 16)
    windows = lax.all_to_all(windows, SUB, 0, 0)
    cot_block = windows.reshape(4, 4, step + 8, out_width).transpose(0, 2, 1, 3)
    cot_block = cot_block.reshape(4, step + 8, group)

    conv_acc = jnp.zeros((lanes, group), f32)
    for columns, weight in ((flat_first, first), (flat_second, second)):
        for k in range(tap_count):
            conv_acc = conv_acc + lax.dot_general(
                columns[k : k + lanes], weight[k], (((1,), (1,)), ((), ())),
                preferred_element_type=f32,
            )
    conv_out = conv_acc.astype(bf16).reshape(4, span, group)
    near = gathered[:, 4 : 4 + rows].reshape(4 * rows, in_width)
    ring = [near] + [turn(near, "y", j) for j in (1, 2, 3)]
    ring = [lax.optimization_barrier(piece.T) for piece in ring]
    conv_out = lax.all_to_all(conv_out, "zl", 0, 0)
    grad, back = statistics(conv_out, cot_block, rows)
    back = lax.all_to_all(back, SUB, 0, 0)
    grad = lax.all_to_all(grad, "zl", 0, 0)

    grad_flat = jnp.concatenate([grad.reshape(lanes, group), jnp.zeros((8, group), bf16)], axis=0)
    sides = []
    for weight in (first, second):
        side = jnp.zeros((lanes, half), f32)
        for k in range(tap_count):
            side = side + jnp.dot(
                grad_flat[4 - k : 4 - k + lanes], weight[k], preferred_element_type=f32
            )
        sides.append(side.astype(bf16))
    running = jnp.where(
        core == 0,
        jnp.concatenate(sides, axis=1),
        jnp.concatenate(sides[::-1], axis=1),
    ).reshape(4, span, in_width)
    own = [
        lax.dynamic_slice(running, ((zl + j) % 4, 0, 0), (1, rows, in_width))[0]
        for j in range(4)
    ]
    parts = own[:1] + [turn(own[j], "zl", j) for j in (1, 2, 3)]
    pooled_grad = sum(part.astype(f32) for part in parts)
    x_float = activations.astype(f32)
    inv_first = lax.rsqrt(jnp.mean(x_float * x_float, axis=1, keepdims=True) + EPSILON)
    normed_first = x_float * inv_first
    slope_first = 0.5 * jnp.repeat(pooled_grad, 2, axis=0)
    slope_first = slope_first * gelu_slope(normed_first, half_erf(normed_first))
    inner_first = jnp.mean(slope_first * normed_first, axis=1, keepdims=True)
    input_grad = (inv_first * (slope_first - normed_first * inner_first)).astype(bf16)

    wide, features = spread_taps(back, tap_count, out_width, rows)
    wide = wide.reshape(4, 4 * rows, tap_count * out_width)
    weight_part = 0.0
    for j in range(4):
        weight_part = weight_part + lax.dot_general(
            ring[j], lax.dynamic_index_in_dim(wide, (y - j) % 4, keepdims=False),
            (((1,), (0,)), ((), ())), preferred_element_type=f32,
        )
    halves = weight_part.reshape(16, 2, in_width // 32, tap_count * out_width)
    mine = jnp.where(core == 0, halves[:, 0], halves[:, 1])
    other = jnp.where(core == 0, halves[:, 1], halves[:, 0]).astype(bf16)
    other = lax.ppermute(other, "core", [(0, 1), (1, 0)])
    total = (mine + other.astype(f32)).astype(bf16)
    total = lax.all_to_all(total, ("zh", "x"), 0, 0)
    weight_grad = jnp.sum(total.astype(f32), axis=0).reshape(-1, tap_count, out_width)
    return (features, input_grad, weight_grad)


def solution(mesh):
    split = Mesh(mesh.devices.reshape(4, 4, 2, 4, 4), AXES)
    return jax.shard_map(
        per_device,
        mesh=split,
        in_specs=(P(AXES, None), P(None, SUB, None), P(SEQ, SUB)),
        out_specs=(P(SEQ, SUB), P(AXES, None), P(SEQ, None, SUB)),
        check_vma=False,
    )
```

```python
import functools

import jax
import jax.numpy as jnp
from jax import lax
from jax.experimental import pallas as pl
from jax.experimental.pallas import tpu as pltpu
from jax.sharding import Mesh, PartitionSpec as P


EPSILON = 1e-06
AXES = ("zh", "x", "core", "zl", "y")
SEQ = ("zh", "x", "core")
SUB = ("zl", "y")
bf16 = jnp.bfloat16
f32 = jnp.float32


def half_erf(tensor):
    return 0.5 * (1.0 + lax.erf(tensor * 0.7071067811865476))


def gelu_slope(tensor, half):
    return half + tensor * jnp.exp(-0.5 * tensor * tensor) * 0.3989422804014327


def shift(block, axis, step):
    count = lax.axis_size(axis)
    pairs = [(i, i + step) for i in range(count) if 0 <= i + step < count]
    return lax.ppermute(block, axis, pairs)


def turn(block, axis, step):
    count = lax.axis_size(axis)
    return lax.ppermute(block, axis, [(i, (i + step) % count) for i in range(count)])


def gather_all(block, axis):
    count = lax.axis_size(axis)
    return lax.all_to_all(jnp.broadcast_to(block, (count, *block.shape)), axis, 0, 0)


def local_call(kernel, shapes, scratch, *args):
    vmem = pl.BlockSpec(memory_space=pltpu.VMEM)
    return pl.pallas_call(
        kernel,
        out_shape=shapes,
        in_specs=[pl.BlockSpec(memory_space=pltpu.SMEM) if a.dtype == jnp.int32 else vmem for a in args],
        out_specs=jax.tree.map(lambda _: vmem, shapes),
        scratch_shapes=scratch,
        compiler_params=pltpu.CompilerParams(vmem_limit_bytes=20 << 20),
    )(*args)


def exact_dot(left, right):
    return jnp.dot(left, right, precision=lax.Precision.HIGHEST, preferred_element_type=f32)


def pair_mean(count, rows, first):
    pair = lax.broadcasted_iota(jnp.int32, (count, rows), 0)
    row = lax.broadcasted_iota(jnp.int32, (count, rows), 1)
    return jnp.where((row - first >= 2 * pair) & (row - first <= 2 * pair + 1), 0.5, 0.0)


def pooled_kernel(low_ref, own_ref, high_ref, out_ref, gelu_ref):
    at = 0
    for ref in (low_ref, own_ref, high_ref):
        count = ref.shape[0]
        wide = ref[...].astype(f32)
        inv = lax.rsqrt(jnp.mean(wide * wide, axis=1, keepdims=True) + EPSILON)
        normed = wide * inv
        gelu_ref[at : at + count, :] = normed * half_erf(normed)
        at += count
    out_ref[...] = exact_dot(pair_mean(at // 2, at, 0), gelu_ref[...]).astype(bf16)


def pooled_block(low, own, high):
    total = low.shape[0] + own.shape[0] + high.shape[0]
    width = own.shape[1]
    return local_call(
        pooled_kernel, jax.ShapeDtypeStruct((total // 2, width), bf16),
        [pltpu.VMEM((total, width), f32)], low, own, high,
    )


def conv_kernel(where_ref, flat_ref, first_ref, second_ref, out_ref, tap_ref):
    lanes = flat_ref.shape[0]
    taps, _, half = first_ref.shape
    core = where_ref[0]
    near = flat_ref[:, pl.ds(pl.multiple_of(core * half, 128), half)]
    far = flat_ref[:, pl.ds(pl.multiple_of((1 - core) * half, 128), half)]
    contract = (((1,), (1,)), ((), ()))
    for k in range(taps):
        tap_ref[k, lanes:, :] = jnp.zeros_like(tap_ref[k, lanes:, :])
        tap_ref[k, :lanes, :] = lax.dot_general(
            near, first_ref[k], contract, preferred_element_type=f32
        ) + lax.dot_general(far, second_ref[k], contract, preferred_element_type=f32)
    total = tap_ref[0, pl.ds(2, lanes), :]
    for k in range(1, taps):
        total = total + tap_ref[k, pl.ds(2 + k, lanes), :]
    out_ref[...] = total.astype(bf16)


def conv_forward(where, flat, first, second):
    taps, group, _ = first.shape
    shape = jax.ShapeDtypeStruct((flat.shape[0], group), bf16)
    scratch = [pltpu.VMEM((taps, flat.shape[0] + 8, group), f32)]
    return local_call(conv_kernel, shape, scratch, where, flat, first, second)


def backward_kernel(rows, where_ref, flat_ref, first_ref, second_ref, *refs):
    out_refs, tap_ref = refs[:4], refs[4]
    taps, _, half = first_ref.shape
    frame = flat_ref.shape[0] // 4
    core, zl = where_ref[0], where_ref[1]
    for side, weight_ref in ((core, first_ref), (1 - core, second_ref)):
        for k in range(taps):
            spread = jnp.dot(flat_ref[...], weight_ref[k], preferred_element_type=f32)
            for f in range(4):
                tap_ref[k, f] = spread[f * frame : (f + 1) * frame]
        for j in range(4):
            f = lax.rem(zl + j, 4)
            total = tap_ref[0, f, pl.ds(10, rows), :]
            for k in range(1, taps):
                total = total + tap_ref[k, f, pl.ds(10 - k, rows), :]
            columns = pl.ds(pl.multiple_of(side * half, 128), half)
            out_refs[j][:, columns] = total.astype(bf16)


def conv_backward(where, flat, first, second, rows):
    taps, _, half = first.shape
    shapes = (jax.ShapeDtypeStruct((rows, 2 * half), bf16),) * 4
    scratch = [pltpu.VMEM((taps, 4, flat.shape[0] // 4, half), f32)]
    kernel = functools.partial(backward_kernel, rows)
    return local_call(kernel, shapes, scratch, where, flat, first, second)


def statistics_kernel(own, y_ref, cot_ref, grad_ref, back_ref):
    groups, _, width = y_ref.shape
    full = groups * width
    pairs = cot_ref.shape[1]
    block = width // 4
    repeat = (
        lax.broadcasted_iota(jnp.int32, (own, pairs), 0) // 2
        == lax.broadcasted_iota(jnp.int32, (own, pairs), 1)
    ).astype(bf16)
    source = lax.broadcasted_iota(jnp.int32, (width, 512), 0)
    lane = lax.broadcasted_iota(jnp.int32, (width, 512), 1)
    spread = ((lane % 128 < block) & (source == lane // 128 * block + lane % 128)).astype(bf16)
    means = pair_mean(pairs, own, 0)
    square = 0.0
    for g in range(groups):
        wide = y_ref[g, :own, :].astype(f32)
        square = square + jnp.sum(wide * wide, axis=1, keepdims=True)
    inv = lax.rsqrt(square / full + EPSILON)
    slopes, inner = [], 0.0
    for g in range(groups):
        normed = y_ref[g, :own, :].astype(f32) * inv
        half = half_erf(normed)
        features = exact_dot(means, normed * half).astype(bf16)
        placed = jnp.dot(features, spread, preferred_element_type=f32).astype(bf16)
        for i in range(4):
            back_ref[4 * g + i, :pairs, :] = placed[:, 128 * i : 128 * i + 128]
        upstream = 0.5 * jnp.dot(repeat, cot_ref[g], preferred_element_type=f32)
        slope = upstream * gelu_slope(normed, half)
        inner = inner + jnp.sum(slope * normed, axis=1, keepdims=True)
        slopes.append(slope)
    mean = inner / full
    for g in range(groups):
        normed = y_ref[g, :own, :].astype(f32) * inv
        grad = (inv * (slopes[g] - normed * mean)).astype(bf16)
        grad_ref[g] = grad
        placed = jnp.dot(grad, spread, preferred_element_type=f32).astype(bf16)
        for i in range(4):
            back_ref[4 * g + i, pairs:, :] = placed[:, 128 * i : 128 * i + 128]


def statistics(conv_out, cot, own):
    groups, _, width = conv_out.shape
    shapes = (
        jax.ShapeDtypeStruct((groups, own, width), bf16),
        jax.ShapeDtypeStruct((4 * groups, own + own // 2, 128), bf16),
    )
    kernel = functools.partial(statistics_kernel, own)
    return local_call(kernel, shapes, [], conv_out, cot)


def weight_kernel(taps, block, where_ref, back_ref, *refs):
    ring_refs, (mine_ref, other_ref, feature_ref, stage_ref, wide_ref, part_ref) = refs[:4], refs[4:]
    count, rows, lanes = back_ref.shape
    pooled = rows // 3
    own = 2 * pooled
    span = wide_ref.shape[1] // 4
    width = wide_ref.shape[2]
    core, y = where_ref[0], where_ref[2]
    source = lax.broadcasted_iota(jnp.int32, (lanes, width), 0)
    lane = lax.broadcasted_iota(jnp.int32, (lanes, width), 1)
    for b in range(count):
        feature_ref[pl.ds(b * pooled, pooled), :] = back_ref[b, :pooled, :block]
    stage_ref[...] = jnp.zeros_like(stage_ref)
    for i in range(4):
        total = jnp.zeros((4 * span, width), f32)
        for k in range(taps):
            for z in range(4):
                stage_ref[pl.ds(z * span + k + 2, own), :] = back_ref[
                    4 * z + i, pooled:, :
                ].astype(f32)
                stage_ref[pl.ds(z * span + k + 1, 1), :] = jnp.zeros((1, lanes), f32)
            place = ((source < block) & (lane == source + k * block)).astype(bf16)
            total = total + jnp.dot(
                stage_ref[...].astype(bf16), place, preferred_element_type=f32
            )
        for z in range(4):
            stage_ref[pl.ds(z * span + taps + 1, own), :] = jnp.zeros((own, lanes), f32)
        wide_ref[i] = total.astype(bf16)
    contract = (((0,), (0,)), ((), ()))
    for j in range(4):
        term = lax.dot_general(
            ring_refs[j][...], wide_ref[lax.rem(y - j + 4, 4)], contract,
            preferred_element_type=f32,
        )
        part_ref[...] = term if j == 0 else part_ref[...] + term
    for c in range(mine_ref.shape[0]):
        step = mine_ref.shape[1]
        near = pl.ds(pl.multiple_of(c * 2 * step + core * step, step), step)
        far = pl.ds(pl.multiple_of(c * 2 * step + (1 - core) * step, step), step)
        mine_ref[c] = part_ref[near, : taps * block]
        other_ref[c] = part_ref[far, : taps * block].astype(bf16)


def weight_partial(where, back, ring, taps, block):
    count, rows, lanes = back.shape
    total, width = ring[0].shape
    lot = (16, width // 32, taps * block)
    wide = (taps * block + 127) // 128 * 128
    shapes = (
        jax.ShapeDtypeStruct(lot, f32),
        jax.ShapeDtypeStruct(lot, bf16),
        jax.ShapeDtypeStruct((count * (rows // 3), block), bf16),
    )
    scratch = [
        pltpu.VMEM((total, lanes), f32),
        pltpu.VMEM((4, total, wide), bf16),
        pltpu.VMEM((width, wide), f32),
    ]
    kernel = functools.partial(weight_kernel, taps, block)
    return local_call(kernel, shapes, scratch, where, back, *ring)


def per_device(activations, conv_weight, cotangent):
    tap_count, out_width, in_width = conv_weight.shape
    core = lax.axis_index("core")
    zl, y = lax.axis_index("zl"), lax.axis_index("y")
    half = in_width // 2
    rows = activations.shape[0] // 2
    span = rows + 8
    group = 4 * out_width
    lanes = 4 * span
    step = rows // 2

    low = shift(activations[-8:], AXES, 1)
    high = shift(activations[:8], AXES, -1)

    own_half = jnp.where(core == 0, conv_weight[:, :, :half], conv_weight[:, :, half:])
    own_half = lax.optimization_barrier(own_half)
    shards = [own_half] + [turn(own_half, "y", j) for j in (1, 2, 3)]
    first = jnp.zeros((tap_count, 4, out_width, half), bf16)
    first = lax.dynamic_update_slice_in_dim(first, shards[0][:, None], y, axis=1)
    for j in range(1, 4):
        first = lax.dynamic_update_slice_in_dim(first, shards[j][:, None], (y - j) % 4, axis=1)
    first = first.reshape(tap_count, group, half)
    second = lax.ppermute(first, "core", [(0, 1), (1, 0)])

    block = pooled_block(low, activations, high)
    gathered = gather_all(block, "zl")
    flat = gathered.reshape(lanes, in_width)
    where = jnp.stack([core, zl, y]).astype(jnp.int32)

    cot, _ = lax.optimization_barrier((cotangent, block))
    cot = lax.all_to_all(cot.reshape(16, step, out_width), SUB, 0, 0)
    cot_block = cot.reshape(4, 4, step, out_width).transpose(0, 2, 1, 3)
    cot_block = cot_block.reshape(4, step, group)

    conv_out = conv_forward(where, flat, first, second).reshape(4, span, group)
    ring = [flat] + [turn(flat, "y", j) for j in (1, 2, 3)]
    conv_out = lax.all_to_all(conv_out, "zl", 0, 0)
    grad, back = statistics(conv_out, cot_block, rows)
    back = lax.all_to_all(back, SUB, 0, 0)
    framed = jnp.concatenate(
        [shift(grad[:, -8:], AXES, 1), grad, shift(grad[:, :8], AXES, -1)], axis=1
    )
    framed = lax.all_to_all(framed, "zl", 0, 0)

    own = conv_backward(where, framed.reshape(-1, group), first, second, rows)
    parts = [own[0]] + [turn(own[j], "zl", j) for j in (1, 2, 3)]
    pooled_grad = sum(part.astype(f32) for part in parts)
    x_float = activations.astype(f32)
    inv_first = lax.rsqrt(jnp.mean(x_float * x_float, axis=1, keepdims=True) + EPSILON)
    normed_first = x_float * inv_first
    slope_first = 0.5 * jnp.repeat(pooled_grad, 2, axis=0)
    slope_first = slope_first * gelu_slope(normed_first, half_erf(normed_first))
    inner_first = jnp.mean(slope_first * normed_first, axis=1, keepdims=True)
    input_grad = (inv_first * (slope_first - normed_first * inner_first)).astype(bf16)

    mine, other, features = weight_partial(where, back, ring, tap_count, out_width)
    other = lax.ppermute(other, "core", [(0, 1), (1, 0)])
    total = (mine + other.astype(f32)).astype(bf16)
    total = lax.all_to_all(total, ("zh", "x"), 0, 0)
    weight_grad = jnp.sum(total.astype(f32), axis=0).reshape(-1, tap_count, out_width)
    return (features, input_grad, weight_grad)


def solution(mesh):
    split = Mesh(mesh.devices.reshape(4, 4, 2, 4, 4), AXES)
    return jax.shard_map(
        per_device,
        mesh=split,
        in_specs=(P(AXES, None), P(None, SUB, None), P(SEQ, SUB)),
        out_specs=(P(SEQ, SUB), P(AXES, None), P(SEQ, None, SUB)),
        check_vma=False,
    )
```

```python
import functools

import jax
import jax.numpy as jnp
from jax import lax
from jax.experimental import pallas as pl
from jax.experimental.pallas import tpu as pltpu
from jax.sharding import Mesh, PartitionSpec as P


EPSILON = 1e-06
AXES = ("zh", "x", "core", "zl", "y")
SEQ = ("zh", "x", "core")
SUB = ("zl", "y")
bf16 = jnp.bfloat16
f32 = jnp.float32


def half_erf(tensor):
    return 0.5 * (1.0 + lax.erf(tensor * 0.7071067811865476))


def gelu_slope(tensor, half):
    return half + tensor * jnp.exp(-0.5 * tensor * tensor) * 0.3989422804014327


def shift(block, axis, step):
    count = lax.axis_size(axis)
    pairs = [(i, i + step) for i in range(count) if 0 <= i + step < count]
    return lax.ppermute(block, axis, pairs)


def turn(block, axis, step):
    count = lax.axis_size(axis)
    return lax.ppermute(block, axis, [(i, (i + step) % count) for i in range(count)])


def gather_all(block, axis):
    count = lax.axis_size(axis)
    return lax.all_to_all(jnp.broadcast_to(block, (count, *block.shape)), axis, 0, 0)


def local_call(kernel, shapes, scratch, *args, limit=12):
    vmem = pl.BlockSpec(memory_space=pltpu.VMEM)
    return pl.pallas_call(
        kernel,
        out_shape=shapes,
        in_specs=[
            pl.BlockSpec(memory_space=pltpu.SMEM) if a.dtype == jnp.int32 else vmem for a in args
        ],
        out_specs=jax.tree.map(lambda _: vmem, shapes),
        scratch_shapes=scratch,
        compiler_params=pltpu.CompilerParams(vmem_limit_bytes=limit << 20),
    )(*args)


def exact_dot(left, right):
    return jnp.dot(left, right, precision=lax.Precision.HIGHEST, preferred_element_type=f32)


def pair_mean(count, rows, first):
    pair = lax.broadcasted_iota(jnp.int32, (count, rows), 0)
    row = lax.broadcasted_iota(jnp.int32, (count, rows), 1)
    return jnp.where((row - first >= 2 * pair) & (row - first <= 2 * pair + 1), 0.5, 0.0)


def pooled_kernel(low_ref, own_ref, high_ref, out_ref, gelu_ref):
    at = 0
    for ref in (low_ref, own_ref, high_ref):
        count = ref.shape[0]
        wide = ref[...].astype(f32)
        inv = lax.rsqrt(jnp.mean(wide * wide, axis=1, keepdims=True) + EPSILON)
        normed = wide * inv
        gelu_ref[at : at + count, :] = normed * half_erf(normed)
        at += count
    out_ref[...] = exact_dot(pair_mean(at // 2, at, 0), gelu_ref[...]).astype(bf16)


def pooled_block(low, own, high):
    total = low.shape[0] + own.shape[0] + high.shape[0]
    width = own.shape[1]
    return local_call(
        pooled_kernel, jax.ShapeDtypeStruct((total // 2, width), bf16),
        [pltpu.VMEM((total, width), f32)], low, own, high,
    )


def conv_kernel(where_ref, flat_ref, first_ref, second_ref, *refs):
    cot_refs, out_ref, tap_ref = refs[:4], refs[4], refs[5]
    lanes = flat_ref.shape[0]
    taps, group, half = first_ref.shape
    core, y = where_ref[0], where_ref[2]
    span = lanes // 4
    own = span - 8
    step, block = cot_refs[0].shape[1:]
    near = flat_ref[:, pl.ds(pl.multiple_of(core * half, 128), half)]
    far = flat_ref[:, pl.ds(pl.multiple_of((1 - core) * half, 128), half)]
    contract = (((1,), (1,)), ((), ()))
    for k in range(taps):
        tap_ref[k, lanes:, :] = jnp.zeros_like(tap_ref[k, lanes:, :])
        tap_ref[k, :lanes, :] = lax.dot_general(
            near, first_ref[k], contract, preferred_element_type=f32
        ) + lax.dot_general(far, second_ref[k], contract, preferred_element_type=f32)
    source = lax.broadcasted_iota(jnp.int32, (block, group), 0)
    lane = lax.broadcasted_iota(jnp.int32, (block, group), 1)
    for f in range(4):
        total = tap_ref[0, pl.ds(f * span + 2, own), :]
        for k in range(1, taps):
            total = total + tap_ref[k, pl.ds(f * span + 2 + k, own), :]
        out_ref[f, :own, :] = total.astype(bf16)
        placed = jnp.zeros((step, group), f32)
        for j in range(4):
            place = (lane == source + lax.rem(y - j + 4, 4) * block).astype(bf16)
            placed = placed + jnp.dot(cot_refs[j][f], place, preferred_element_type=f32)
        out_ref[f, own:, :] = placed.astype(bf16)


def conv_forward(where, flat, first, second, cots):
    taps, group, _ = first.shape
    span = flat.shape[0] // 4
    shape = jax.ShapeDtypeStruct((4, span - 8 + cots[0].shape[1], group), bf16)
    scratch = [pltpu.VMEM((taps, flat.shape[0] + 8, group), f32)]
    return local_call(conv_kernel, shape, scratch, where, flat, first, second, *cots)


def backward_kernel(rows, where_ref, flat_ref, first_ref, second_ref, *refs):
    out_refs, tap_ref = refs[:4], refs[4]
    taps, _, half = first_ref.shape
    frame = flat_ref.shape[0] // 4
    core, zl = where_ref[0], where_ref[1]
    for side, weight_ref in ((core, first_ref), (1 - core, second_ref)):
        for k in range(taps):
            spread = jnp.dot(flat_ref[...], weight_ref[k], preferred_element_type=f32)
            for f in range(4):
                tap_ref[k, f] = spread[f * frame : (f + 1) * frame]
        for j in range(4):
            f = lax.rem(zl + j, 4)
            total = tap_ref[0, f, pl.ds(10, rows), :]
            for k in range(1, taps):
                total = total + tap_ref[k, f, pl.ds(10 - k, rows), :]
            columns = pl.ds(pl.multiple_of(side * half, 128), half)
            out_refs[j][:, columns] = total.astype(bf16)


def conv_backward(where, flat, first, second, rows):
    taps, _, half = first.shape
    shapes = (jax.ShapeDtypeStruct((rows, 2 * half), bf16),) * 4
    scratch = [pltpu.VMEM((taps, 4, flat.shape[0] // 4, half), f32)]
    kernel = functools.partial(backward_kernel, rows)
    return local_call(kernel, shapes, scratch, where, flat, first, second, limit=16)


def statistics_kernel(own, y_ref, grad_ref, back_ref, head_ref, tail_ref):
    groups, _, width = y_ref.shape
    full = groups * width
    pairs = own // 2
    block = width // 4
    repeat = (
        lax.broadcasted_iota(jnp.int32, (own, pairs), 0) // 2
        == lax.broadcasted_iota(jnp.int32, (own, pairs), 1)
    ).astype(bf16)
    source = lax.broadcasted_iota(jnp.int32, (width, 512), 0)
    lane = lax.broadcasted_iota(jnp.int32, (width, 512), 1)
    spread = ((lane % 128 < block) & (source == lane // 128 * block + lane % 128)).astype(bf16)
    means = pair_mean(pairs, own, 0)
    square = 0.0
    for g in range(groups):
        wide = y_ref[g, :own, :].astype(f32)
        square = square + jnp.sum(wide * wide, axis=1, keepdims=True)
    inv = lax.rsqrt(square / full + EPSILON)
    slopes, inner = [], 0.0
    for g in range(groups):
        normed = y_ref[g, :own, :].astype(f32) * inv
        half = half_erf(normed)
        features = exact_dot(means, normed * half).astype(bf16)
        placed = jnp.dot(features, spread, preferred_element_type=f32).astype(bf16)
        for i in range(4):
            back_ref[4 * g + i, :pairs, :] = placed[:, 128 * i : 128 * i + 128]
        upstream = 0.5 * jnp.dot(repeat, y_ref[g, own:, :], preferred_element_type=f32)
        slope = upstream * gelu_slope(normed, half)
        inner = inner + jnp.sum(slope * normed, axis=1, keepdims=True)
        slopes.append(slope)
    mean = inner / full
    for g in range(groups):
        normed = y_ref[g, :own, :].astype(f32) * inv
        grad = (inv * (slopes[g] - normed * mean)).astype(bf16)
        grad_ref[g] = grad
        head_ref[g] = grad_ref[g, :8, :]
        tail_ref[g] = grad_ref[g, own - 8 :, :]
        placed = jnp.dot(grad, spread, preferred_element_type=f32).astype(bf16)
        for i in range(4):
            back_ref[4 * g + i, pairs:, :] = placed[:, 128 * i : 128 * i + 128]


def statistics(conv_out, own):
    groups, _, width = conv_out.shape
    shapes = (
        jax.ShapeDtypeStruct((groups, own, width), bf16),
        jax.ShapeDtypeStruct((4 * groups, own + own // 2, 128), bf16),
        jax.ShapeDtypeStruct((groups, 8, width), bf16),
        jax.ShapeDtypeStruct((groups, 8, width), bf16),
    )
    kernel = functools.partial(statistics_kernel, own)
    return local_call(kernel, shapes, [], conv_out)


def input_kernel(act_ref, *refs):
    part_refs, out_ref = refs[:4], refs[4]
    rows = act_ref.shape[0]
    pooled_grad = sum(ref[...].astype(f32) for ref in part_refs)
    pair = lax.broadcasted_iota(jnp.int32, (rows, rows // 2), 1)
    row = lax.broadcasted_iota(jnp.int32, (rows, rows // 2), 0)
    upstream = exact_dot(jnp.where(row // 2 == pair, 0.5, 0.0), pooled_grad)
    wide = act_ref[...].astype(f32)
    inv = lax.rsqrt(jnp.mean(wide * wide, axis=1, keepdims=True) + EPSILON)
    normed = wide * inv
    slope = upstream * gelu_slope(normed, half_erf(normed))
    inner = jnp.mean(slope * normed, axis=1, keepdims=True)
    out_ref[...] = (inv * (slope - normed * inner)).astype(bf16)


def input_gradient(activations, parts):
    shape = jax.ShapeDtypeStruct(activations.shape, bf16)
    return local_call(input_kernel, shape, [], activations, *parts)


def weight_kernel(taps, block, where_ref, back_ref, *refs):
    ring_refs, (mine_ref, other_ref, feature_ref, stage_ref, wide_ref, part_ref) = refs[:5], refs[5:]
    count, rows, lanes = back_ref.shape
    pooled = rows // 3
    own = 2 * pooled
    span = wide_ref.shape[1] // 4
    width = wide_ref.shape[2]
    core, y = where_ref[0], where_ref[2]
    source = lax.broadcasted_iota(jnp.int32, (lanes, width), 0)
    lane = lax.broadcasted_iota(jnp.int32, (lanes, width), 1)
    for b in range(count):
        feature_ref[pl.ds(b * pooled, pooled), :] = back_ref[b, :pooled, :block]
    stage_ref[...] = jnp.zeros_like(stage_ref)
    for i in range(4):
        total = jnp.zeros((4 * span, width), f32)
        for k in range(taps):
            for z in range(4):
                stage_ref[pl.ds(z * span + k + 2, own), :] = back_ref[
                    4 * z + i, pooled:, :
                ].astype(f32)
                stage_ref[pl.ds(z * span + k + 1, 1), :] = jnp.zeros((1, lanes), f32)
            place = ((source < block) & (lane == source + k * block)).astype(bf16)
            total = total + jnp.dot(
                stage_ref[...].astype(bf16), place, preferred_element_type=f32
            )
        for z in range(4):
            stage_ref[pl.ds(z * span + taps + 1, own), :] = jnp.zeros((own, lanes), f32)
        wide_ref[i] = total.astype(bf16)
    contract = (((0,), (0,)), ((), ()))
    middle = 2 * span
    pieces = ((0, slice(None)), (3, slice(None)), (1, slice(None)), (2, slice(0, middle)), (2, slice(middle, None)))
    for ref, (turns, some) in zip(ring_refs, pieces, strict=True):
        term = lax.dot_general(
            ref[...], wide_ref[lax.rem(y + turns, 4), some], contract,
            preferred_element_type=f32,
        )
        part_ref[...] = term if ref is ring_refs[0] else part_ref[...] + term
    for c in range(mine_ref.shape[0]):
        step = mine_ref.shape[1]
        near = pl.ds(pl.multiple_of(c * 2 * step + core * step, step), step)
        far = pl.ds(pl.multiple_of(c * 2 * step + (1 - core) * step, step), step)
        mine_ref[c] = part_ref[near, : taps * block]
        other_ref[c] = part_ref[far, : taps * block].astype(bf16)


def weight_partial(where, back, ring, taps, block):
    count, rows, lanes = back.shape
    total, width = ring[0].shape
    lot = (16, width // 32, taps * block)
    wide = (taps * block + 127) // 128 * 128
    shapes = (
        jax.ShapeDtypeStruct(lot, f32),
        jax.ShapeDtypeStruct(lot, bf16),
        jax.ShapeDtypeStruct((count * (rows // 3), block), bf16),
    )
    scratch = [
        pltpu.VMEM((total, lanes), f32),
        pltpu.VMEM((4, total, wide), bf16),
        pltpu.VMEM((width, wide), f32),
    ]
    kernel = functools.partial(weight_kernel, taps, block)
    return local_call(kernel, shapes, scratch, where, back, *ring, limit=16)


def per_device(activations, conv_weight, cotangent):
    tap_count, out_width, in_width = conv_weight.shape
    core = lax.axis_index("core")
    zl, y = lax.axis_index("zl"), lax.axis_index("y")
    half = in_width // 2
    rows = activations.shape[0] // 2
    span = rows + 8
    group = 4 * out_width
    lanes = 4 * span
    step = rows // 2

    low = shift(activations[-8:], AXES, 1)
    high = shift(activations[:8], AXES, -1)

    own_half = jnp.where(core == 0, conv_weight[:, :, :half], conv_weight[:, :, half:])
    own_half = lax.optimization_barrier(own_half)
    shards = [own_half] + [turn(own_half, "y", j) for j in (1, 2, 3)]
    first = jnp.zeros((tap_count, 4, out_width, half), bf16)
    first = lax.dynamic_update_slice_in_dim(first, shards[0][:, None], y, axis=1)
    for j in range(1, 4):
        first = lax.dynamic_update_slice_in_dim(first, shards[j][:, None], (y - j) % 4, axis=1)
    first = first.reshape(tap_count, group, half)
    second = lax.ppermute(first, "core", [(0, 1), (1, 0)])

    block = pooled_block(low, activations, high)
    gathered = gather_all(block, "zl")
    flat = gathered.reshape(lanes, in_width)
    where = jnp.stack([core, zl, y]).astype(jnp.int32)

    cot, _ = lax.optimization_barrier((cotangent, block))
    cot = cot.reshape(4, 4, step, out_width)
    cots = [lax.dynamic_index_in_dim(cot, (y + j) % 4, 1, keepdims=False) for j in range(4)]
    cots = cots[:1] + [turn(cots[j], "y", j) for j in (1, 2, 3)]

    conv_out = conv_forward(where, flat, first, second, cots)
    up, down = turn(flat, "y", 1), turn(flat, "y", -1)
    far = [turn(up[: 2 * span], "y", 1), turn(down[2 * span :], "y", -1)]
    conv_out = lax.all_to_all(conv_out, "zl", 0, 0)
    grad, back, head, tail = statistics(conv_out, rows)
    back = lax.all_to_all(back, SUB, 0, 0)
    tail, head = shift(tail, AXES, 1), shift(head, AXES, -1)
    framed = jnp.concatenate([tail, grad, head], axis=1)
    framed = lax.all_to_all(framed, "zl", 0, 0)

    own = conv_backward(where, framed.reshape(-1, group), first, second, rows)
    parts = [own[0], turn(own[2], "zl", 2)]
    parts = parts + [turn(own[1], "zl", 1), turn(own[3], "zl", 3)]
    input_grad = input_gradient(activations, parts)

    mine, other, features = weight_partial(
        where, back, [flat, up, down, *far], tap_count, out_width
    )
    other = lax.ppermute(other, "core", [(0, 1), (1, 0)])
    total = (mine + other.astype(f32)).astype(bf16)
    total = lax.all_to_all(total, ("zh", "x"), 0, 0)
    weight_grad = jnp.sum(total.astype(f32), axis=0).reshape(-1, tap_count, out_width)
    return (features, input_grad, weight_grad)


def solution(mesh):
    split = Mesh(mesh.devices.reshape(4, 4, 2, 4, 4), AXES)
    return jax.shard_map(
        per_device,
        mesh=split,
        in_specs=(P(AXES, None), P(None, SUB, None), P(SEQ, SUB)),
        out_specs=(P(SEQ, SUB), P(AXES, None), P(SEQ, None, SUB)),
        check_vma=False,
    )
```

```python
import functools

import jax
import jax.numpy as jnp
from jax import lax
from jax.experimental import pallas as pl
from jax.experimental.pallas import tpu as pltpu
from jax.sharding import Mesh, PartitionSpec as P


EPSILON = 1e-06
AXES = ("zh", "x", "core", "zl", "y")
SEQ = ("zh", "x", "core")
SUB = ("zl", "y")
bf16 = jnp.bfloat16
f32 = jnp.float32


def half_erf(tensor):
    return 0.5 * (1.0 + lax.erf(tensor * 0.7071067811865476))


def gelu_slope(tensor, half):
    return half + tensor * jnp.exp(-0.5 * tensor * tensor) * 0.3989422804014327


def shift(block, axis, step):
    count = lax.axis_size(axis)
    pairs = [(i, i + step) for i in range(count) if 0 <= i + step < count]
    return lax.ppermute(block, axis, pairs)


def turn(block, axis, step):
    count = lax.axis_size(axis)
    return lax.ppermute(block, axis, [(i, (i + step) % count) for i in range(count)])


def gather_all(block, axis):
    count = lax.axis_size(axis)
    return lax.all_to_all(jnp.broadcast_to(block, (count, *block.shape)), axis, 0, 0)


def local_call(kernel, shapes, scratch, *args, limit=12):
    vmem = pl.BlockSpec(memory_space=pltpu.VMEM)
    return pl.pallas_call(
        kernel,
        out_shape=shapes,
        in_specs=[
            pl.BlockSpec(memory_space=pltpu.SMEM) if a.dtype == jnp.int32 else vmem for a in args
        ],
        out_specs=jax.tree.map(lambda _: vmem, shapes),
        scratch_shapes=scratch,
        compiler_params=pltpu.CompilerParams(vmem_limit_bytes=limit << 20),
    )(*args)


def exact_dot(left, right):
    return jnp.dot(left, right, precision=lax.Precision.HIGHEST, preferred_element_type=f32)


def pair_mean(count, rows, first):
    pair = lax.broadcasted_iota(jnp.int32, (count, rows), 0)
    row = lax.broadcasted_iota(jnp.int32, (count, rows), 1)
    return jnp.where((row - first >= 2 * pair) & (row - first <= 2 * pair + 1), 0.5, 0.0)


def pooled_kernel(low_ref, own_ref, high_ref, out_ref, gelu_ref):
    at = 0
    for ref in (low_ref, own_ref, high_ref):
        count = ref.shape[0]
        wide = ref[...].astype(f32)
        inv = lax.rsqrt(jnp.mean(wide * wide, axis=1, keepdims=True) + EPSILON)
        normed = wide * inv
        gelu_ref[at : at + count, :] = normed * half_erf(normed)
        at += count
    out_ref[...] = exact_dot(pair_mean(at // 2, at, 0), gelu_ref[...]).astype(bf16)


def pooled_block(low, own, high):
    total = low.shape[0] + own.shape[0] + high.shape[0]
    width = own.shape[1]
    return local_call(
        pooled_kernel, jax.ShapeDtypeStruct((total // 2, width), bf16),
        [pltpu.VMEM((total, width), f32)], low, own, high,
    )


def conv_kernel(where_ref, flat_ref, first_ref, second_ref, *refs):
    cot_refs, out_ref, tap_ref = refs[:4], refs[4], refs[5]
    lanes = flat_ref.shape[0]
    taps, group, half = first_ref.shape
    core, y = where_ref[0], where_ref[2]
    span = lanes // 4
    own = span - 8
    step, block = cot_refs[0].shape[1:]
    near = flat_ref[:, pl.ds(pl.multiple_of(core * half, 128), half)]
    far = flat_ref[:, pl.ds(pl.multiple_of((1 - core) * half, 128), half)]
    contract = (((1,), (1,)), ((), ()))
    for k in range(taps):
        tap_ref[k, lanes:, :] = jnp.zeros_like(tap_ref[k, lanes:, :])
        tap_ref[k, :lanes, :] = lax.dot_general(
            near, first_ref[k], contract, preferred_element_type=f32
        ) + lax.dot_general(far, second_ref[k], contract, preferred_element_type=f32)
    source = lax.broadcasted_iota(jnp.int32, (block, group), 0)
    lane = lax.broadcasted_iota(jnp.int32, (block, group), 1)
    for f in range(4):
        total = tap_ref[0, pl.ds(f * span + 2, own), :]
        for k in range(1, taps):
            total = total + tap_ref[k, pl.ds(f * span + 2 + k, own), :]
        out_ref[f, :own, :] = total.astype(bf16)
        placed = jnp.zeros((step, group), f32)
        for j in range(4):
            place = (lane == source + lax.rem(y - j + 4, 4) * block).astype(bf16)
            placed = placed + jnp.dot(cot_refs[j][f], place, preferred_element_type=f32)
        out_ref[f, own:, :] = placed.astype(bf16)


def conv_forward(where, flat, first, second, cots):
    taps, group, _ = first.shape
    span = flat.shape[0] // 4
    shape = jax.ShapeDtypeStruct((4, span - 8 + cots[0].shape[1], group), bf16)
    scratch = [pltpu.VMEM((taps, flat.shape[0] + 8, group), f32)]
    return local_call(conv_kernel, shape, scratch, where, flat, first, second, *cots)


def backward_kernel(rows, where_ref, flat_ref, first_ref, second_ref, *refs):
    out_refs, tap_ref = refs[:4], refs[4]
    taps, _, half = first_ref.shape
    frame = flat_ref.shape[0] // 4
    core, zl = where_ref[0], where_ref[1]
    for side, weight_ref in ((core, first_ref), (1 - core, second_ref)):
        for k in range(taps):
            spread = jnp.dot(flat_ref[...], weight_ref[k], preferred_element_type=f32)
            for f in range(4):
                tap_ref[k, f] = spread[f * frame : (f + 1) * frame]
        for j in range(4):
            f = lax.rem(zl + j, 4)
            total = tap_ref[0, f, pl.ds(10, rows), :]
            for k in range(1, taps):
                total = total + tap_ref[k, f, pl.ds(10 - k, rows), :]
            columns = pl.ds(pl.multiple_of(side * half, 128), half)
            out_refs[j][:, columns] = total.astype(bf16)


def conv_backward(where, flat, first, second, rows):
    taps, _, half = first.shape
    shapes = (jax.ShapeDtypeStruct((rows, 2 * half), bf16),) * 4
    scratch = [pltpu.VMEM((taps, 4, flat.shape[0] // 4, half), f32)]
    kernel = functools.partial(backward_kernel, rows)
    return local_call(kernel, shapes, scratch, where, flat, first, second, limit=16)


def statistics_kernel(own, y_ref, grad_ref, back_ref, head_ref, tail_ref):
    groups, _, width = y_ref.shape
    full = groups * width
    pairs = own // 2
    block = width // 4
    repeat = (
        lax.broadcasted_iota(jnp.int32, (own, pairs), 0) // 2
        == lax.broadcasted_iota(jnp.int32, (own, pairs), 1)
    ).astype(bf16)
    source = lax.broadcasted_iota(jnp.int32, (width, 512), 0)
    lane = lax.broadcasted_iota(jnp.int32, (width, 512), 1)
    spread = ((lane % 128 < block) & (source == lane // 128 * block + lane % 128)).astype(bf16)
    means = pair_mean(pairs, own, 0)
    square = 0.0
    for g in range(groups):
        wide = y_ref[g, :own, :].astype(f32)
        square = square + jnp.sum(wide * wide, axis=1, keepdims=True)
    inv = lax.rsqrt(square / full + EPSILON)
    slopes, inner = [], 0.0
    for g in range(groups):
        normed = y_ref[g, :own, :].astype(f32) * inv
        half = half_erf(normed)
        features = exact_dot(means, normed * half).astype(bf16)
        placed = jnp.dot(features, spread, preferred_element_type=f32).astype(bf16)
        for i in range(4):
            back_ref[4 * g + i, :pairs, :] = placed[:, 128 * i : 128 * i + 128]
        upstream = 0.5 * jnp.dot(repeat, y_ref[g, own:, :], preferred_element_type=f32)
        slope = upstream * gelu_slope(normed, half)
        inner = inner + jnp.sum(slope * normed, axis=1, keepdims=True)
        slopes.append(slope)
    mean = inner / full
    for g in range(groups):
        normed = y_ref[g, :own, :].astype(f32) * inv
        grad = (inv * (slopes[g] - normed * mean)).astype(bf16)
        grad_ref[g] = grad
        head_ref[g] = grad_ref[g, :8, :]
        tail_ref[g] = grad_ref[g, own - 8 :, :]
        placed = jnp.dot(grad, spread, preferred_element_type=f32).astype(bf16)
        for i in range(4):
            back_ref[4 * g + i, pairs:, :] = placed[:, 128 * i : 128 * i + 128]


def statistics(conv_out, own):
    groups, _, width = conv_out.shape
    shapes = (
        jax.ShapeDtypeStruct((groups, own, width), bf16),
        jax.ShapeDtypeStruct((4 * groups, own + own // 2, 128), bf16),
        jax.ShapeDtypeStruct((groups, 8, width), bf16),
        jax.ShapeDtypeStruct((groups, 8, width), bf16),
    )
    kernel = functools.partial(statistics_kernel, own)
    return local_call(kernel, shapes, [], conv_out)


def input_kernel(act_ref, *refs):
    part_refs, out_ref = refs[:4], refs[4]
    rows = act_ref.shape[0]
    pooled_grad = sum(ref[...].astype(f32) for ref in part_refs)
    pair = lax.broadcasted_iota(jnp.int32, (rows, rows // 2), 1)
    row = lax.broadcasted_iota(jnp.int32, (rows, rows // 2), 0)
    upstream = exact_dot(jnp.where(row // 2 == pair, 0.5, 0.0), pooled_grad)
    wide = act_ref[...].astype(f32)
    inv = lax.rsqrt(jnp.mean(wide * wide, axis=1, keepdims=True) + EPSILON)
    normed = wide * inv
    slope = upstream * gelu_slope(normed, half_erf(normed))
    inner = jnp.mean(slope * normed, axis=1, keepdims=True)
    out_ref[...] = (inv * (slope - normed * inner)).astype(bf16)


def input_gradient(activations, parts):
    shape = jax.ShapeDtypeStruct(activations.shape, bf16)
    return local_call(input_kernel, shape, [], activations, *parts)


def weight_kernel(taps, block, where_ref, back_ref, *refs):
    ring_refs, (mine_ref, other_ref, feature_ref, stage_ref, wide_ref, part_ref) = refs[:4], refs[4:]
    count, rows, lanes = back_ref.shape
    pooled = rows // 3
    own = 2 * pooled
    span = wide_ref.shape[1] // 4
    width = wide_ref.shape[2]
    core, y = where_ref[0], where_ref[2]
    source = lax.broadcasted_iota(jnp.int32, (lanes, width), 0)
    lane = lax.broadcasted_iota(jnp.int32, (lanes, width), 1)
    for b in range(count):
        feature_ref[pl.ds(b * pooled, pooled), :] = back_ref[b, :pooled, :block]
    stage_ref[...] = jnp.zeros_like(stage_ref)
    for i in range(4):
        total = jnp.zeros((4 * span, width), f32)
        for k in range(taps):
            for z in range(4):
                stage_ref[pl.ds(z * span + k + 2, own), :] = back_ref[
                    4 * z + i, pooled:, :
                ].astype(f32)
                stage_ref[pl.ds(z * span + k + 1, 1), :] = jnp.zeros((1, lanes), f32)
            place = ((source < block) & (lane == source + k * block)).astype(bf16)
            total = total + jnp.dot(
                stage_ref[...].astype(bf16), place, preferred_element_type=f32
            )
        for z in range(4):
            stage_ref[pl.ds(z * span + taps + 1, own), :] = jnp.zeros((own, lanes), f32)
        wide_ref[i] = total.astype(bf16)
    contract = (((0,), (0,)), ((), ()))
    for j, turns in enumerate((0, 3, 1, 2)):
        term = lax.dot_general(
            ring_refs[j][...], wide_ref[lax.rem(y + turns, 4)], contract,
            preferred_element_type=f32,
        )
        part_ref[...] = term if j == 0 else part_ref[...] + term
    for c in range(mine_ref.shape[0]):
        step = mine_ref.shape[1]
        near = pl.ds(pl.multiple_of(c * 2 * step + core * step, step), step)
        far = pl.ds(pl.multiple_of(c * 2 * step + (1 - core) * step, step), step)
        mine_ref[c] = part_ref[near, : taps * block]
        other_ref[c] = part_ref[far, : taps * block].astype(bf16)


def weight_partial(where, back, ring, taps, block):
    count, rows, lanes = back.shape
    total, width = ring[0].shape
    lot = (16, width // 32, taps * block)
    wide = (taps * block + 127) // 128 * 128
    shapes = (
        jax.ShapeDtypeStruct(lot, f32),
        jax.ShapeDtypeStruct(lot, bf16),
        jax.ShapeDtypeStruct((count * (rows // 3), block), bf16),
    )
    scratch = [
        pltpu.VMEM((total, lanes), f32),
        pltpu.VMEM((4, total, wide), bf16),
        pltpu.VMEM((width, wide), f32),
    ]
    kernel = functools.partial(weight_kernel, taps, block)
    return local_call(kernel, shapes, scratch, where, back, *ring, limit=16)


def per_device(activations, conv_weight, cotangent):
    tap_count, out_width, in_width = conv_weight.shape
    core = lax.axis_index("core")
    zl, y = lax.axis_index("zl"), lax.axis_index("y")
    half = in_width // 2
    rows = activations.shape[0] // 2
    span = rows + 8
    group = 4 * out_width
    lanes = 4 * span
    step = rows // 2

    low = shift(activations[-8:], AXES, 1)
    high = shift(activations[:8], AXES, -1)

    own_half = jnp.where(core == 0, conv_weight[:, :, :half], conv_weight[:, :, half:])
    own_half = lax.optimization_barrier(own_half)
    shards = [own_half] + [turn(own_half, "y", j) for j in (1, 2, 3)]
    first = jnp.zeros((tap_count, 4, out_width, half), bf16)
    first = lax.dynamic_update_slice_in_dim(first, shards[0][:, None], y, axis=1)
    for j in range(1, 4):
        first = lax.dynamic_update_slice_in_dim(first, shards[j][:, None], (y - j) % 4, axis=1)
    first = first.reshape(tap_count, group, half)
    second = lax.ppermute(first, "core", [(0, 1), (1, 0)])

    block = pooled_block(low, activations, high)
    gathered = gather_all(block, "zl")
    flat = gathered.reshape(lanes, in_width)
    where = jnp.stack([core, zl, y]).astype(jnp.int32)

    cot, _ = lax.optimization_barrier((cotangent, block))
    cot = cot.reshape(4, 4, step, out_width)
    cots = [lax.dynamic_index_in_dim(cot, (y + j) % 4, 1, keepdims=False) for j in range(4)]
    cots = cots[:1] + [turn(cots[j], "y", j) for j in (1, 2, 3)]

    conv_out = conv_forward(where, flat, first, second, cots)
    up, down = turn(flat, "y", 1), turn(flat, "y", -1)
    far = turn(flat, "y", 2)
    conv_out = lax.all_to_all(conv_out, "zl", 0, 0)
    grad, back, head, tail = statistics(conv_out, rows)
    back = lax.all_to_all(back, SUB, 0, 0)
    tail, head = shift(tail, AXES, 1), shift(head, AXES, -1)
    framed = jnp.concatenate([tail, grad, head], axis=1)
    framed = lax.all_to_all(framed, "zl", 0, 0)

    own = conv_backward(where, framed.reshape(-1, group), first, second, rows)
    parts = [own[0], turn(own[2], "zl", 2)]
    parts = parts + [turn(own[1], "zl", 1), turn(own[3], "zl", 3)]
    input_grad = input_gradient(activations, parts)

    mine, other, features = weight_partial(
        where, back, [flat, up, down, far], tap_count, out_width
    )
    other = lax.ppermute(other, "core", [(0, 1), (1, 0)])
    total = (mine + other.astype(f32)).astype(bf16)
    total = lax.all_to_all(total, ("zh", "x"), 0, 0)
    weight_grad = jnp.sum(total.astype(f32), axis=0).reshape(-1, tap_count, out_width)
    return (features, input_grad, weight_grad)


def solution(mesh):
    split = Mesh(mesh.devices.reshape(4, 4, 2, 4, 4), AXES)
    return jax.shard_map(
        per_device,
        mesh=split,
        in_specs=(P(AXES, None), P(None, SUB, None), P(SEQ, SUB)),
        out_specs=(P(SEQ, SUB), P(AXES, None), P(SEQ, None, SUB)),
        check_vma=False,
    )
```

```python
import functools

import jax
import jax.numpy as jnp
from jax import lax
from jax.experimental import pallas as pl
from jax.experimental.pallas import tpu as pltpu
from jax.sharding import Mesh, PartitionSpec as P


EPSILON = 1e-06
AXES = ("zh", "x", "core", "zl", "y")
SEQ = ("zh", "x", "core")
SUB = ("zl", "y")
bf16 = jnp.bfloat16
f32 = jnp.float32


def half_erf(tensor):
    return 0.5 * (1.0 + lax.erf(tensor * 0.7071067811865476))


def gelu_slope(tensor, half):
    return half + tensor * jnp.exp(-0.5 * tensor * tensor) * 0.3989422804014327


def shift(block, axis, step):
    count = lax.axis_size(axis)
    pairs = [(i, i + step) for i in range(count) if 0 <= i + step < count]
    return lax.ppermute(block, axis, pairs)


def turn(block, axis, step):
    count = lax.axis_size(axis)
    return lax.ppermute(block, axis, [(i, (i + step) % count) for i in range(count)])


def gather_all(block, axis):
    count = lax.axis_size(axis)
    return lax.all_to_all(jnp.broadcast_to(block, (count, *block.shape)), axis, 0, 0)


def local_call(kernel, shapes, scratch, *args, limit=12):
    vmem = pl.BlockSpec(memory_space=pltpu.VMEM)
    return pl.pallas_call(
        kernel,
        out_shape=shapes,
        in_specs=[
            pl.BlockSpec(memory_space=pltpu.SMEM) if a.dtype == jnp.int32 else vmem for a in args
        ],
        out_specs=jax.tree.map(lambda _: vmem, shapes),
        scratch_shapes=scratch,
        compiler_params=pltpu.CompilerParams(vmem_limit_bytes=limit << 20),
    )(*args)


def exact_dot(left, right):
    return jnp.dot(left, right, precision=lax.Precision.HIGHEST, preferred_element_type=f32)


def pair_mean(count, rows, first):
    pair = lax.broadcasted_iota(jnp.int32, (count, rows), 0)
    row = lax.broadcasted_iota(jnp.int32, (count, rows), 1)
    return jnp.where((row - first >= 2 * pair) & (row - first <= 2 * pair + 1), 0.5, 0.0)


def pooled_kernel(low_ref, own_ref, high_ref, out_ref, gelu_ref):
    at = 0
    for ref in (low_ref, own_ref, high_ref):
        count = ref.shape[0]
        wide = ref[...].astype(f32)
        inv = lax.rsqrt(jnp.mean(wide * wide, axis=1, keepdims=True) + EPSILON)
        normed = wide * inv
        gelu_ref[at : at + count, :] = normed * half_erf(normed)
        at += count
    out_ref[...] = exact_dot(pair_mean(at // 2, at, 0), gelu_ref[...]).astype(bf16)


def pooled_block(low, own, high):
    total = low.shape[0] + own.shape[0] + high.shape[0]
    width = own.shape[1]
    return local_call(
        pooled_kernel, jax.ShapeDtypeStruct((total // 2, width), bf16),
        [pltpu.VMEM((total, width), f32)], low, own, high,
    )


def conv_kernel(where_ref, flat_ref, first_ref, second_ref, *refs):
    cot_refs, out_ref, tap_ref = refs[:4], refs[4], refs[5]
    lanes = flat_ref.shape[0]
    taps, group, half = first_ref.shape
    core, y = where_ref[0], where_ref[2]
    span = lanes // 4
    own = span - 8
    step, block = cot_refs[0].shape[1:]
    near = flat_ref[:, pl.ds(pl.multiple_of(core * half, 128), half)]
    far = flat_ref[:, pl.ds(pl.multiple_of((1 - core) * half, 128), half)]
    contract = (((1,), (1,)), ((), ()))
    for k in range(taps):
        tap_ref[k, lanes:, :] = jnp.zeros_like(tap_ref[k, lanes:, :])
        tap_ref[k, :lanes, :] = lax.dot_general(
            near, first_ref[k], contract, preferred_element_type=f32
        ) + lax.dot_general(far, second_ref[k], contract, preferred_element_type=f32)
    source = lax.broadcasted_iota(jnp.int32, (block, group), 0)
    lane = lax.broadcasted_iota(jnp.int32, (block, group), 1)
    for f in range(4):
        total = tap_ref[0, pl.ds(f * span + 2, own), :]
        for k in range(1, taps):
            total = total + tap_ref[k, pl.ds(f * span + 2 + k, own), :]
        out_ref[f, :own, :] = total.astype(bf16)
        placed = jnp.zeros((step, group), f32)
        for j in range(4):
            place = (lane == source + lax.rem(y - j + 4, 4) * block).astype(bf16)
            placed = placed + jnp.dot(cot_refs[j][f], place, preferred_element_type=f32)
        out_ref[f, own:, :] = placed.astype(bf16)


def conv_forward(where, flat, first, second, cots):
    taps, group, _ = first.shape
    span = flat.shape[0] // 4
    shape = jax.ShapeDtypeStruct((4, span - 8 + cots[0].shape[1], group), bf16)
    scratch = [pltpu.VMEM((taps, flat.shape[0] + 8, group), f32)]
    return local_call(conv_kernel, shape, scratch, where, flat, first, second, *cots)


def backward_kernel(rows, where_ref, flat_ref, first_ref, second_ref, *refs):
    out_refs, tap_ref = refs[:4], refs[4]
    taps, _, half = first_ref.shape
    frame = flat_ref.shape[0] // 4
    core, zl = where_ref[0], where_ref[1]
    for side, weight_ref in ((core, first_ref), (1 - core, second_ref)):
        for k in range(taps):
            spread = jnp.dot(flat_ref[...], weight_ref[k], preferred_element_type=f32)
            for f in range(4):
                tap_ref[k, f] = spread[f * frame : (f + 1) * frame]
        for j in range(4):
            f = lax.rem(zl + j, 4)
            total = tap_ref[0, f, pl.ds(10, rows), :]
            for k in range(1, taps):
                total = total + tap_ref[k, f, pl.ds(10 - k, rows), :]
            columns = pl.ds(pl.multiple_of(side * half, 128), half)
            out_refs[j][:, columns] = total.astype(bf16)


def conv_backward(where, flat, first, second, rows):
    taps, _, half = first.shape
    shapes = (jax.ShapeDtypeStruct((rows, 2 * half), bf16),) * 4
    scratch = [pltpu.VMEM((taps, 4, flat.shape[0] // 4, half), f32)]
    kernel = functools.partial(backward_kernel, rows)
    return local_call(kernel, shapes, scratch, where, flat, first, second, limit=16)


def statistics_kernel(own, y_ref, grad_ref, back_ref, edge_ref):
    groups, _, width = y_ref.shape
    full = groups * width
    pairs = own // 2
    block = width // 4
    repeat = (
        lax.broadcasted_iota(jnp.int32, (own, pairs), 0) // 2
        == lax.broadcasted_iota(jnp.int32, (own, pairs), 1)
    ).astype(bf16)
    source = lax.broadcasted_iota(jnp.int32, (width, 512), 0)
    lane = lax.broadcasted_iota(jnp.int32, (width, 512), 1)
    spread = ((lane % 128 < block) & (source == lane // 128 * block + lane % 128)).astype(bf16)
    means = pair_mean(pairs, own, 0)
    square = 0.0
    for g in range(groups):
        wide = y_ref[g, :own, :].astype(f32)
        square = square + jnp.sum(wide * wide, axis=1, keepdims=True)
    inv = lax.rsqrt(square / full + EPSILON)
    slopes, inner = [], 0.0
    for g in range(groups):
        normed = y_ref[g, :own, :].astype(f32) * inv
        half = half_erf(normed)
        features = exact_dot(means, normed * half).astype(bf16)
        placed = jnp.dot(features, spread, preferred_element_type=f32).astype(bf16)
        for i in range(4):
            back_ref[4 * g + i, :pairs, :] = placed[:, 128 * i : 128 * i + 128]
        upstream = 0.5 * jnp.dot(repeat, y_ref[g, own:, :], preferred_element_type=f32)
        slope = upstream * gelu_slope(normed, half)
        inner = inner + jnp.sum(slope * normed, axis=1, keepdims=True)
        slopes.append(slope)
    mean = inner / full
    for g in range(groups):
        normed = y_ref[g, :own, :].astype(f32) * inv
        grad = (inv * (slopes[g] - normed * mean)).astype(bf16)
        grad_ref[g] = grad
        edge_ref[0, g] = grad_ref[g, :8, :]
        edge_ref[1, g] = grad_ref[g, own - 8 :, :]
        placed = jnp.dot(grad, spread, preferred_element_type=f32).astype(bf16)
        for i in range(4):
            back_ref[4 * g + i, pairs:, :] = placed[:, 128 * i : 128 * i + 128]


def statistics(conv_out, own):
    groups, _, width = conv_out.shape
    shapes = (
        jax.ShapeDtypeStruct((groups, own, width), bf16),
        jax.ShapeDtypeStruct((4 * groups, own + own // 2, 128), bf16),
        jax.ShapeDtypeStruct((2, groups, 8, width), bf16),
    )
    kernel = functools.partial(statistics_kernel, own)
    return local_call(kernel, shapes, [], conv_out)


def input_kernel(act_ref, *refs):
    part_refs, out_ref = refs[:4], refs[4]
    rows = act_ref.shape[0]
    pooled_grad = sum(ref[...].astype(f32) for ref in part_refs)
    pair = lax.broadcasted_iota(jnp.int32, (rows, rows // 2), 1)
    row = lax.broadcasted_iota(jnp.int32, (rows, rows // 2), 0)
    upstream = exact_dot(jnp.where(row // 2 == pair, 0.5, 0.0), pooled_grad)
    wide = act_ref[...].astype(f32)
    inv = lax.rsqrt(jnp.mean(wide * wide, axis=1, keepdims=True) + EPSILON)
    normed = wide * inv
    slope = upstream * gelu_slope(normed, half_erf(normed))
    inner = jnp.mean(slope * normed, axis=1, keepdims=True)
    out_ref[...] = (inv * (slope - normed * inner)).astype(bf16)


def input_gradient(activations, parts):
    shape = jax.ShapeDtypeStruct(activations.shape, bf16)
    return local_call(input_kernel, shape, [], activations, *parts)


def weight_kernel(taps, block, where_ref, back_ref, *refs):
    ring_refs, (mine_ref, other_ref, feature_ref, stage_ref, wide_ref, part_ref) = refs[:4], refs[4:]
    count, rows, lanes = back_ref.shape
    pooled = rows // 3
    own = 2 * pooled
    span = wide_ref.shape[1] // 4
    width = wide_ref.shape[2]
    core, y = where_ref[0], where_ref[2]
    source = lax.broadcasted_iota(jnp.int32, (lanes, width), 0)
    lane = lax.broadcasted_iota(jnp.int32, (lanes, width), 1)
    for b in range(count):
        feature_ref[pl.ds(b * pooled, pooled), :] = back_ref[b, :pooled, :block]
    stage_ref[...] = jnp.zeros_like(stage_ref)
    for i in range(4):
        total = jnp.zeros((4 * span, width), f32)
        for k in range(taps):
            for z in range(4):
                stage_ref[pl.ds(z * span + k + 2, own), :] = back_ref[
                    4 * z + i, pooled:, :
                ].astype(f32)
                stage_ref[pl.ds(z * span + k + 1, 1), :] = jnp.zeros((1, lanes), f32)
            place = ((source < block) & (lane == source + k * block)).astype(bf16)
            total = total + jnp.dot(
                stage_ref[...].astype(bf16), place, preferred_element_type=f32
            )
        for z in range(4):
            stage_ref[pl.ds(z * span + taps + 1, own), :] = jnp.zeros((own, lanes), f32)
        wide_ref[i] = total.astype(bf16)
    contract = (((0,), (0,)), ((), ()))
    for j, turns in enumerate((0, 3, 1, 2)):
        term = lax.dot_general(
            ring_refs[j][...], wide_ref[lax.rem(y + turns, 4)], contract,
            preferred_element_type=f32,
        )
        part_ref[...] = term if j == 0 else part_ref[...] + term
    for c in range(mine_ref.shape[0]):
        step = mine_ref.shape[1]
        near = pl.ds(pl.multiple_of(c * 2 * step + core * step, step), step)
        far = pl.ds(pl.multiple_of(c * 2 * step + (1 - core) * step, step), step)
        mine_ref[c] = part_ref[near, : taps * block]
        other_ref[c] = part_ref[far, : taps * block].astype(bf16)


def weight_partial(where, back, ring, taps, block):
    count, rows, lanes = back.shape
    total, width = ring[0].shape
    lot = (16, width // 32, taps * block)
    wide = (taps * block + 127) // 128 * 128
    shapes = (
        jax.ShapeDtypeStruct(lot, f32),
        jax.ShapeDtypeStruct(lot, bf16),
        jax.ShapeDtypeStruct((count * (rows // 3), block), bf16),
    )
    scratch = [
        pltpu.VMEM((total, lanes), f32),
        pltpu.VMEM((4, total, wide), bf16),
        pltpu.VMEM((width, wide), f32),
    ]
    kernel = functools.partial(weight_kernel, taps, block)
    return local_call(kernel, shapes, scratch, where, back, *ring, limit=16)


def per_device(activations, conv_weight, cotangent):
    tap_count, out_width, in_width = conv_weight.shape
    core = lax.axis_index("core")
    zl, y = lax.axis_index("zl"), lax.axis_index("y")
    half = in_width // 2
    rows = activations.shape[0] // 2
    span = rows + 8
    group = 4 * out_width
    lanes = 4 * span
    step = rows // 2

    low = shift(activations[-8:], AXES, 1)
    high = shift(activations[:8], AXES, -1)

    own_half = jnp.where(core == 0, conv_weight[:, :, :half], conv_weight[:, :, half:])
    own_half = lax.optimization_barrier(own_half)
    shards = [own_half] + [turn(own_half, "y", j) for j in (1, 2, 3)]
    first = jnp.zeros((tap_count, 4, out_width, half), bf16)
    first = lax.dynamic_update_slice_in_dim(first, shards[0][:, None], y, axis=1)
    for j in range(1, 4):
        first = lax.dynamic_update_slice_in_dim(first, shards[j][:, None], (y - j) % 4, axis=1)
    first = first.reshape(tap_count, group, half)
    second = lax.ppermute(first, "core", [(0, 1), (1, 0)])

    block = pooled_block(low, activations, high)
    gathered = gather_all(block, "zl")
    flat = gathered.reshape(lanes, in_width)
    where = jnp.stack([core, zl, y]).astype(jnp.int32)

    cot, _ = lax.optimization_barrier((cotangent, block))
    cot = cot.reshape(4, 4, step, out_width)
    cots = [lax.dynamic_index_in_dim(cot, (y + j) % 4, 1, keepdims=False) for j in range(4)]
    cots = cots[:1] + [turn(cots[j], "y", j) for j in (1, 2, 3)]

    conv_out = conv_forward(where, flat, first, second, cots)
    up, down = turn(flat, "y", 1), turn(flat, "y", -1)
    far = turn(flat, "y", 2)
    conv_out = lax.all_to_all(conv_out, "zl", 0, 0)
    grad, back, edge = statistics(conv_out, rows)
    back = lax.all_to_all(back, SUB, 0, 0)
    low, high = shift(edge, AXES, 1), shift(edge, AXES, -1)
    framed = jnp.concatenate([low[1], grad, high[0]], axis=1)
    framed = lax.all_to_all(framed, "zl", 0, 0)

    own = conv_backward(where, framed.reshape(-1, group), first, second, rows)
    parts = [own[0], turn(own[2], "zl", 2)]
    parts = parts + [turn(own[1], "zl", 1), turn(own[3], "zl", 3)]
    input_grad = input_gradient(activations, parts)

    mine, other, features = weight_partial(
        where, back, [flat, up, down, far], tap_count, out_width
    )
    other = lax.ppermute(other, "core", [(0, 1), (1, 0)])
    total = (mine + other.astype(f32)).astype(bf16)
    total = lax.all_to_all(total, ("zh", "x"), 0, 0)
    weight_grad = jnp.sum(total.astype(f32), axis=0).reshape(-1, tap_count, out_width)
    return (features, input_grad, weight_grad)


def solution(mesh):
    split = Mesh(mesh.devices.reshape(4, 4, 2, 4, 4), AXES)
    return jax.shard_map(
        per_device,
        mesh=split,
        in_specs=(P(AXES, None), P(None, SUB, None), P(SEQ, SUB)),
        out_specs=(P(SEQ, SUB), P(AXES, None), P(SEQ, None, SUB)),
        check_vma=False,
    )
```

```python
import functools

import jax
import jax.numpy as jnp
from jax import lax
from jax.experimental import pallas as pl
from jax.experimental.pallas import tpu as pltpu
from jax.sharding import Mesh, PartitionSpec as P


EPSILON = 1e-06
AXES = ("zh", "x", "core", "zl", "y")
SEQ = ("zh", "x", "core")
SUB = ("zl", "y")
bf16 = jnp.bfloat16
f32 = jnp.float32


def half_erf(tensor):
    return 0.5 * (1.0 + lax.erf(tensor * 0.7071067811865476))


def gelu_slope(tensor, half):
    return half + tensor * jnp.exp(-0.5 * tensor * tensor) * 0.3989422804014327


def shift(block, axis, step):
    count = lax.axis_size(axis)
    pairs = [(i, i + step) for i in range(count) if 0 <= i + step < count]
    return lax.ppermute(block, axis, pairs)


def turn(block, axis, step):
    count = lax.axis_size(axis)
    return lax.ppermute(block, axis, [(i, (i + step) % count) for i in range(count)])


def gather_all(block, axis):
    count = lax.axis_size(axis)
    return lax.all_to_all(jnp.broadcast_to(block, (count, *block.shape)), axis, 0, 0)


def local_call(kernel, shapes, scratch, *args, limit=12):
    vmem = pl.BlockSpec(memory_space=pltpu.VMEM)
    return pl.pallas_call(
        kernel,
        out_shape=shapes,
        in_specs=[
            pl.BlockSpec(memory_space=pltpu.SMEM) if a.dtype == jnp.int32 else vmem for a in args
        ],
        out_specs=jax.tree.map(lambda _: vmem, shapes),
        scratch_shapes=scratch,
        compiler_params=pltpu.CompilerParams(vmem_limit_bytes=limit << 20),
    )(*args)


def exact_dot(left, right):
    return jnp.dot(left, right, precision=lax.Precision.HIGHEST, preferred_element_type=f32)


def pair_mean(count, rows, first):
    pair = lax.broadcasted_iota(jnp.int32, (count, rows), 0)
    row = lax.broadcasted_iota(jnp.int32, (count, rows), 1)
    return jnp.where((row - first >= 2 * pair) & (row - first <= 2 * pair + 1), 0.5, 0.0)


def pooled_kernel(low_ref, own_ref, high_ref, out_ref, gelu_ref):
    at = 0
    for ref in (low_ref, own_ref, high_ref):
        count = ref.shape[0]
        wide = ref[...].astype(f32)
        inv = lax.rsqrt(jnp.mean(wide * wide, axis=1, keepdims=True) + EPSILON)
        normed = wide * inv
        gelu_ref[at : at + count, :] = normed * half_erf(normed)
        at += count
    out_ref[...] = exact_dot(pair_mean(at // 2, at, 0), gelu_ref[...]).astype(bf16)


def pooled_block(low, own, high):
    total = low.shape[0] + own.shape[0] + high.shape[0]
    width = own.shape[1]
    return local_call(
        pooled_kernel, jax.ShapeDtypeStruct((total // 2, width), bf16),
        [pltpu.VMEM((total, width), f32)], low, own, high,
    )


def conv_kernel(where_ref, flat_ref, first_ref, second_ref, *refs):
    cot_refs, out_ref, tap_ref = refs[:4], refs[4], refs[5]
    lanes = flat_ref.shape[0]
    taps, group, half = first_ref.shape
    core, y = where_ref[0], where_ref[2]
    span = lanes // 4
    own = span - 8
    step, block = cot_refs[0].shape[1:]
    near = flat_ref[:, pl.ds(pl.multiple_of(core * half, 128), half)]
    far = flat_ref[:, pl.ds(pl.multiple_of((1 - core) * half, 128), half)]
    contract = (((1,), (1,)), ((), ()))
    for k in range(taps):
        tap_ref[k, lanes:, :] = jnp.zeros_like(tap_ref[k, lanes:, :])
        tap_ref[k, :lanes, :] = lax.dot_general(
            near, first_ref[k], contract, preferred_element_type=f32
        ) + lax.dot_general(far, second_ref[k], contract, preferred_element_type=f32)
    source = lax.broadcasted_iota(jnp.int32, (block, group), 0)
    lane = lax.broadcasted_iota(jnp.int32, (block, group), 1)
    for f in range(4):
        total = tap_ref[0, pl.ds(f * span + 2, own), :]
        for k in range(1, taps):
            total = total + tap_ref[k, pl.ds(f * span + 2 + k, own), :]
        out_ref[f, :own, :] = total.astype(bf16)
        placed = jnp.zeros((step, group), f32)
        for j in range(4):
            place = (lane == source + lax.rem(y - j + 4, 4) * block).astype(bf16)
            placed = placed + jnp.dot(cot_refs[j][f], place, preferred_element_type=f32)
        out_ref[f, own:, :] = placed.astype(bf16)


def conv_forward(where, flat, first, second, cots):
    taps, group, _ = first.shape
    span = flat.shape[0] // 4
    shape = jax.ShapeDtypeStruct((4, span - 8 + cots[0].shape[1], group), bf16)
    scratch = [pltpu.VMEM((taps, flat.shape[0] + 8, group), f32)]
    return local_call(conv_kernel, shape, scratch, where, flat, first, second, *cots)


def backward_kernel(rows, where_ref, flat_ref, first_ref, second_ref, *refs):
    out_refs, tap_ref = refs[:4], refs[4]
    taps, _, half = first_ref.shape
    frame = flat_ref.shape[0] // 4
    core, zl = where_ref[0], where_ref[1]
    for side, weight_ref in ((core, first_ref), (1 - core, second_ref)):
        for k in range(taps):
            spread = jnp.dot(flat_ref[...], weight_ref[k], preferred_element_type=f32)
            for f in range(4):
                tap_ref[k, f] = spread[f * frame : (f + 1) * frame]
        for j in range(4):
            f = lax.rem(zl + j, 4)
            total = tap_ref[0, f, pl.ds(10, rows), :]
            for k in range(1, taps):
                total = total + tap_ref[k, f, pl.ds(10 - k, rows), :]
            columns = pl.ds(pl.multiple_of(side * half, 128), half)
            out_refs[j][:, columns] = total.astype(bf16)


def conv_backward(where, flat, first, second, rows):
    taps, _, half = first.shape
    shapes = (jax.ShapeDtypeStruct((rows, 2 * half), bf16),) * 4
    scratch = [pltpu.VMEM((taps, 4, flat.shape[0] // 4, half), f32)]
    kernel = functools.partial(backward_kernel, rows)
    return local_call(kernel, shapes, scratch, where, flat, first, second, limit=16)


def statistics_kernel(own, y_ref, grad_ref, back_ref, head_ref, tail_ref):
    groups, _, width = y_ref.shape
    full = groups * width
    pairs = own // 2
    block = width // 4
    repeat = (
        lax.broadcasted_iota(jnp.int32, (own, pairs), 0) // 2
        == lax.broadcasted_iota(jnp.int32, (own, pairs), 1)
    ).astype(bf16)
    source = lax.broadcasted_iota(jnp.int32, (width, 512), 0)
    lane = lax.broadcasted_iota(jnp.int32, (width, 512), 1)
    spread = ((lane % 128 < block) & (source == lane // 128 * block + lane % 128)).astype(bf16)
    means = pair_mean(pairs, own, 0)
    square = 0.0
    for g in range(groups):
        wide = y_ref[g, :own, :].astype(f32)
        square = square + jnp.sum(wide * wide, axis=1, keepdims=True)
    inv = lax.rsqrt(square / full + EPSILON)
    slopes, inner = [], 0.0
    for g in range(groups):
        normed = y_ref[g, :own, :].astype(f32) * inv
        half = half_erf(normed)
        features = exact_dot(means, normed * half).astype(bf16)
        placed = jnp.dot(features, spread, preferred_element_type=f32).astype(bf16)
        for i in range(4):
            back_ref[4 * g + i, :pairs, :] = placed[:, 128 * i : 128 * i + 128]
        upstream = 0.5 * jnp.dot(repeat, y_ref[g, own:, :], preferred_element_type=f32)
        slope = upstream * gelu_slope(normed, half)
        inner = inner + jnp.sum(slope * normed, axis=1, keepdims=True)
        slopes.append(slope)
    mean = inner / full
    for g in range(groups):
        normed = y_ref[g, :own, :].astype(f32) * inv
        grad = (inv * (slopes[g] - normed * mean)).astype(bf16)
        grad_ref[g] = grad
        head_ref[g] = grad_ref[g, :8, :]
        tail_ref[g] = grad_ref[g, own - 8 :, :]
        placed = jnp.dot(grad, spread, preferred_element_type=f32).astype(bf16)
        for i in range(4):
            back_ref[4 * g + i, pairs:, :] = placed[:, 128 * i : 128 * i + 128]


def statistics(conv_out, own):
    groups, _, width = conv_out.shape
    shapes = (
        jax.ShapeDtypeStruct((groups, own, width), bf16),
        jax.ShapeDtypeStruct((4 * groups, own + own // 2, 128), bf16),
        jax.ShapeDtypeStruct((groups, 8, width), bf16),
        jax.ShapeDtypeStruct((groups, 8, width), bf16),
    )
    kernel = functools.partial(statistics_kernel, own)
    return local_call(kernel, shapes, [], conv_out)


def input_kernel(act_ref, *refs):
    part_refs, out_ref = refs[:4], refs[4]
    rows = act_ref.shape[0]
    pooled_grad = sum(ref[...].astype(f32) for ref in part_refs)
    pair = lax.broadcasted_iota(jnp.int32, (rows, rows // 2), 1)
    row = lax.broadcasted_iota(jnp.int32, (rows, rows // 2), 0)
    upstream = exact_dot(jnp.where(row // 2 == pair, 0.5, 0.0), pooled_grad)
    wide = act_ref[...].astype(f32)
    inv = lax.rsqrt(jnp.mean(wide * wide, axis=1, keepdims=True) + EPSILON)
    normed = wide * inv
    slope = upstream * gelu_slope(normed, half_erf(normed))
    inner = jnp.mean(slope * normed, axis=1, keepdims=True)
    out_ref[...] = (inv * (slope - normed * inner)).astype(bf16)


def input_gradient(activations, parts):
    shape = jax.ShapeDtypeStruct(activations.shape, bf16)
    return local_call(input_kernel, shape, [], activations, *parts)


def weight_kernel(taps, block, where_ref, back_ref, *refs):
    ring_refs, (mine_ref, other_ref, feature_ref, stage_ref, wide_ref, part_ref) = refs[:4], refs[4:]
    count, rows, lanes = back_ref.shape
    pooled = rows // 3
    own = 2 * pooled
    span = wide_ref.shape[1] // 4
    width = wide_ref.shape[2]
    core, y = where_ref[0], where_ref[2]
    source = lax.broadcasted_iota(jnp.int32, (lanes, width), 0)
    lane = lax.broadcasted_iota(jnp.int32, (lanes, width), 1)
    for b in range(count):
        feature_ref[pl.ds(b * pooled, pooled), :] = back_ref[b, :pooled, :block]
    stage_ref[...] = jnp.zeros_like(stage_ref)
    for i in range(4):
        total = jnp.zeros((4 * span, width), f32)
        for k in range(taps):
            for z in range(4):
                stage_ref[pl.ds(z * span + k + 2, own), :] = back_ref[
                    4 * z + i, pooled:, :
                ].astype(f32)
                stage_ref[pl.ds(z * span + k + 1, 1), :] = jnp.zeros((1, lanes), f32)
            place = ((source < block) & (lane == source + k * block)).astype(bf16)
            total = total + jnp.dot(
                stage_ref[...].astype(bf16), place, preferred_element_type=f32
            )
        for z in range(4):
            stage_ref[pl.ds(z * span + taps + 1, own), :] = jnp.zeros((own, lanes), f32)
        wide_ref[i] = total.astype(bf16)
    contract = (((0,), (0,)), ((), ()))
    for j, turns in enumerate((0, 3, 1, 2)):
        term = lax.dot_general(
            ring_refs[j][...], wide_ref[lax.rem(y + turns, 4)], contract,
            preferred_element_type=f32,
        )
        part_ref[...] = term if j == 0 else part_ref[...] + term
    for c in range(mine_ref.shape[0]):
        step = mine_ref.shape[1]
        near = pl.ds(pl.multiple_of(c * 2 * step + core * step, step), step)
        far = pl.ds(pl.multiple_of(c * 2 * step + (1 - core) * step, step), step)
        at = c % 4 * 4 + c // 4
        mine_ref[at] = part_ref[near, : taps * block]
        other_ref[at] = part_ref[far, : taps * block].astype(bf16)


def weight_partial(where, back, ring, taps, block):
    count, rows, lanes = back.shape
    total, width = ring[0].shape
    lot = (16, width // 32, taps * block)
    wide = (taps * block + 127) // 128 * 128
    shapes = (
        jax.ShapeDtypeStruct(lot, f32),
        jax.ShapeDtypeStruct(lot, bf16),
        jax.ShapeDtypeStruct((count * (rows // 3), block), bf16),
    )
    scratch = [
        pltpu.VMEM((total, lanes), f32),
        pltpu.VMEM((4, total, wide), bf16),
        pltpu.VMEM((width, wide), f32),
    ]
    kernel = functools.partial(weight_kernel, taps, block)
    return local_call(kernel, shapes, scratch, where, back, *ring, limit=16)


def per_device(activations, conv_weight, cotangent):
    tap_count, out_width, in_width = conv_weight.shape
    core = lax.axis_index("core")
    zl, y = lax.axis_index("zl"), lax.axis_index("y")
    half = in_width // 2
    rows = activations.shape[0] // 2
    span = rows + 8
    group = 4 * out_width
    lanes = 4 * span
    step = rows // 2

    low = shift(activations[-8:], AXES, 1)
    high = shift(activations[:8], AXES, -1)

    own_half = jnp.where(core == 0, conv_weight[:, :, :half], conv_weight[:, :, half:])
    own_half = lax.optimization_barrier(own_half)
    shards = [own_half] + [turn(own_half, "y", j) for j in (1, 2, 3)]
    first = jnp.zeros((tap_count, 4, out_width, half), bf16)
    first = lax.dynamic_update_slice_in_dim(first, shards[0][:, None], y, axis=1)
    for j in range(1, 4):
        first = lax.dynamic_update_slice_in_dim(first, shards[j][:, None], (y - j) % 4, axis=1)
    first = first.reshape(tap_count, group, half)
    second = lax.ppermute(first, "core", [(0, 1), (1, 0)])

    block = pooled_block(low, activations, high)
    gathered = gather_all(block, "zl")
    flat = gathered.reshape(lanes, in_width)
    where = jnp.stack([core, zl, y]).astype(jnp.int32)

    cot, _ = lax.optimization_barrier((cotangent, block))
    cot = cot.reshape(4, 4, step, out_width)
    cots = [lax.dynamic_index_in_dim(cot, (y + j) % 4, 1, keepdims=False) for j in range(4)]
    cots = cots[:1] + [turn(cots[j], "y", j) for j in (1, 2, 3)]

    conv_out = conv_forward(where, flat, first, second, cots)
    up, down = turn(flat, "y", 1), turn(flat, "y", -1)
    far = turn(flat, "y", 2)
    conv_out = lax.all_to_all(conv_out, "zl", 0, 0)
    grad, back, head, tail = statistics(conv_out, rows)
    back = lax.all_to_all(back, SUB, 0, 0)
    tail, head = shift(tail, AXES, 1), shift(head, AXES, -1)
    framed = jnp.concatenate([tail, grad, head], axis=1)
    framed = lax.all_to_all(framed, "zl", 0, 0)

    own = conv_backward(where, framed.reshape(-1, group), first, second, rows)
    parts = [own[0], turn(own[2], "zl", 2)]
    parts = parts + [turn(own[1], "zl", 1), turn(own[3], "zl", 3)]
    input_grad = input_gradient(activations, parts)

    mine, other, features = weight_partial(where, back, [flat, up, down, far], tap_count, out_width)
    other = lax.ppermute(other, "core", [(0, 1), (1, 0)])
    total = (mine + other.astype(f32)).astype(bf16)
    zh = lax.axis_index("zh")
    total = lax.all_to_all(total.reshape(4, 4, *total.shape[1:]), "x", 0, 0)
    total = jnp.sum(total.astype(f32), axis=0)
    upper = zh // 2
    away = lax.dynamic_slice_in_dim(total, 2 - 2 * upper, 2).astype(bf16)
    away = lax.ppermute(away, "zh", [(i, i ^ 2) for i in range(4)])
    total = lax.dynamic_slice_in_dim(total, 2 * upper, 2) + away.astype(f32)
    lower = zh % 2
    away = lax.dynamic_index_in_dim(total, 1 - lower, keepdims=False).astype(bf16)
    away = lax.ppermute(away, "zh", [(i, i ^ 1) for i in range(4)])
    total = lax.dynamic_index_in_dim(total, lower, keepdims=False) + away.astype(f32)
    weight_grad = total.reshape(-1, tap_count, out_width)
    return (features, input_grad, weight_grad)


def solution(mesh):
    split = Mesh(mesh.devices.reshape(4, 4, 2, 4, 4), AXES)
    return jax.shard_map(
        per_device,
        mesh=split,
        in_specs=(P(AXES, None), P(None, SUB, None), P(SEQ, SUB)),
        out_specs=(P(SEQ, SUB), P(AXES, None), P(SEQ, None, SUB)),
        check_vma=False,
    )
```

```python
import functools

import jax
import jax.numpy as jnp
from jax import lax
from jax.experimental import pallas as pl
from jax.experimental.pallas import tpu as pltpu
from jax.sharding import Mesh, PartitionSpec as P


EPSILON = 1e-06
AXES = ("zh", "x", "core", "zl", "y")
SEQ = ("zh", "x", "core")
SUB = ("zl", "y")
bf16 = jnp.bfloat16
f32 = jnp.float32


def half_erf(tensor):
    return 0.5 * (1.0 + lax.erf(tensor * 0.7071067811865476))


def gelu_slope(tensor, half):
    return half + tensor * jnp.exp(-0.5 * tensor * tensor) * 0.3989422804014327


def shift(block, axis, step):
    count = lax.axis_size(axis)
    pairs = [(i, i + step) for i in range(count) if 0 <= i + step < count]
    return lax.ppermute(block, axis, pairs)


def turn(block, axis, step):
    count = lax.axis_size(axis)
    return lax.ppermute(block, axis, [(i, (i + step) % count) for i in range(count)])


def gather_all(block, axis):
    count = lax.axis_size(axis)
    return lax.all_to_all(jnp.broadcast_to(block, (count, *block.shape)), axis, 0, 0)


def local_call(kernel, shapes, scratch, *args, limit=12):
    vmem = pl.BlockSpec(memory_space=pltpu.VMEM)
    return pl.pallas_call(
        kernel,
        out_shape=shapes,
        in_specs=[
            pl.BlockSpec(memory_space=pltpu.SMEM) if a.dtype == jnp.int32 else vmem for a in args
        ],
        out_specs=jax.tree.map(lambda _: vmem, shapes),
        scratch_shapes=scratch,
        compiler_params=pltpu.CompilerParams(vmem_limit_bytes=limit << 20),
    )(*args)


def exact_dot(left, right):
    return jnp.dot(left, right, precision=lax.Precision.HIGHEST, preferred_element_type=f32)


def pair_mean(count, rows, first):
    pair = lax.broadcasted_iota(jnp.int32, (count, rows), 0)
    row = lax.broadcasted_iota(jnp.int32, (count, rows), 1)
    return jnp.where((row - first >= 2 * pair) & (row - first <= 2 * pair + 1), 0.5, 0.0)


def pooled_kernel(low_ref, own_ref, high_ref, out_ref, gelu_ref):
    at = 0
    for ref in (low_ref, own_ref, high_ref):
        count = ref.shape[0]
        wide = ref[...].astype(f32)
        inv = lax.rsqrt(jnp.mean(wide * wide, axis=1, keepdims=True) + EPSILON)
        normed = wide * inv
        gelu_ref[at : at + count, :] = normed * half_erf(normed)
        at += count
    out_ref[...] = exact_dot(pair_mean(at // 2, at, 0), gelu_ref[...]).astype(bf16)


def pooled_block(low, own, high):
    total = low.shape[0] + own.shape[0] + high.shape[0]
    width = own.shape[1]
    return local_call(
        pooled_kernel, jax.ShapeDtypeStruct((total // 2, width), bf16),
        [pltpu.VMEM((total, width), f32)], low, own, high,
    )


def pack_kernel(where_ref, weight_ref, cot_ref, own_ref, *pack_refs):
    taps, block, width = weight_ref.shape
    step = own_ref.shape[0]
    half = width // 2
    core, y = where_ref[0], where_ref[2]
    for j, ref in enumerate((own_ref, *pack_refs)):
        ref[:step, :] = jnp.zeros((step, half), bf16)
        for f in range(4):
            at = pl.multiple_of((f * 4 + lax.rem(y + j, 4)) * step, step)
            ref[:step, 128 * f : 128 * f + block] = cot_ref[pl.ds(at, step), :]
    for k in range(taps):
        piece = weight_ref[k, :, pl.ds(pl.multiple_of(core * half, 128), half)]
        for ref in pack_refs:
            ref[step + k * block : step + (k + 1) * block, :] = piece


def pack_shards(where, weight, cot):
    taps, block, width = weight.shape
    step = cot.shape[0] // 16
    shapes = (jax.ShapeDtypeStruct((step, width // 2), bf16),) + (
        jax.ShapeDtypeStruct((step + taps * block, width // 2), bf16),
    ) * 3
    return local_call(pack_kernel, shapes, [], where, weight, cot)


def conv_kernel(where_ref, flat_ref, first_ref, second_ref, *refs):
    own_ref, pack_refs, (out_ref, tap_ref, cot_ref, done) = refs[0], refs[1:4], refs[4:]
    lanes = flat_ref.shape[0]
    taps, group, half = first_ref.shape
    core, y = where_ref[0], where_ref[2]
    span = lanes // 4
    own = span - 8
    step, block = own_ref.shape[0], group // 4
    copies = [
        pltpu.make_async_copy(pack_refs[j].at[pl.ds(0, step), :], cot_ref.at[j], done.at[j])
        for j in range(3)
    ]
    for copy in copies:
        copy.start()
    near = flat_ref[:, pl.ds(pl.multiple_of(core * half, 128), half)]
    far = flat_ref[:, pl.ds(pl.multiple_of((1 - core) * half, 128), half)]
    contract = (((1,), (1,)), ((), ()))
    for k in range(taps):
        tap_ref[k, lanes:, :] = jnp.zeros_like(tap_ref[k, lanes:, :])
        tap_ref[k, :lanes, :] = lax.dot_general(
            near, first_ref[k], contract, preferred_element_type=f32
        ) + lax.dot_general(far, second_ref[k], contract, preferred_element_type=f32)
    for copy in copies:
        copy.wait()
    cots = [own_ref[...]] + [cot_ref[j] for j in range(3)]
    source = lax.broadcasted_iota(jnp.int32, (block, group), 0)
    lane = lax.broadcasted_iota(jnp.int32, (block, group), 1)
    for f in range(4):
        total = tap_ref[0, pl.ds(f * span + 2, own), :]
        for k in range(1, taps):
            total = total + tap_ref[k, pl.ds(f * span + 2 + k, own), :]
        out_ref[f, :own, :] = total.astype(bf16)
        placed = jnp.zeros((step, group), f32)
        for j in range(4):
            place = (lane == source + lax.rem(y - j + 4, 4) * block).astype(bf16)
            placed = placed + jnp.dot(
                cots[j][:, 128 * f : 128 * f + block], place, preferred_element_type=f32
            )
        out_ref[f, own:, :] = placed.astype(bf16)


def conv_forward(where, flat, first, second, own, packs):
    taps, group, _ = first.shape
    span = flat.shape[0] // 4
    vmem, hbm = pl.BlockSpec(memory_space=pltpu.VMEM), pl.BlockSpec(memory_space=pl.ANY)
    return pl.pallas_call(
        conv_kernel,
        out_shape=jax.ShapeDtypeStruct((4, span - 8 + own.shape[0], group), bf16),
        in_specs=[pl.BlockSpec(memory_space=pltpu.SMEM)] + [vmem] * 4 + [hbm] * 3,
        out_specs=vmem,
        scratch_shapes=[
            pltpu.VMEM((taps, flat.shape[0] + 8, group), f32),
            pltpu.VMEM((3, *own.shape), bf16),
            pltpu.SemaphoreType.DMA((3,)),
        ],
        compiler_params=pltpu.CompilerParams(vmem_limit_bytes=12 << 20),
        name="conv_forward",
    )(where, flat, first, second, own, *packs)


def backward_kernel(rows, where_ref, flat_ref, first_ref, second_ref, *refs):
    out_refs, tap_ref = refs[:4], refs[4]
    taps, _, half = first_ref.shape
    frame = flat_ref.shape[0] // 4
    core, zl = where_ref[0], where_ref[1]
    for side, weight_ref in ((core, first_ref), (1 - core, second_ref)):
        for k in range(taps):
            spread = jnp.dot(flat_ref[...], weight_ref[k], preferred_element_type=f32)
            for f in range(4):
                tap_ref[k, f] = spread[f * frame : (f + 1) * frame]
        for j in range(4):
            f = lax.rem(zl + j, 4)
            total = tap_ref[0, f, pl.ds(10, rows), :]
            for k in range(1, taps):
                total = total + tap_ref[k, f, pl.ds(10 - k, rows), :]
            columns = pl.ds(pl.multiple_of(side * half, 128), half)
            out_refs[j][:, columns] = total.astype(bf16)


def conv_backward(where, flat, first, second, rows):
    taps, _, half = first.shape
    shapes = (jax.ShapeDtypeStruct((rows, 2 * half), bf16),) * 4
    scratch = [pltpu.VMEM((taps, 4, flat.shape[0] // 4, half), f32)]
    kernel = functools.partial(backward_kernel, rows)
    return local_call(kernel, shapes, scratch, where, flat, first, second, limit=16)


def statistics_kernel(own, y_ref, grad_ref, back_ref, head_ref, tail_ref):
    groups, _, width = y_ref.shape
    full = groups * width
    pairs = own // 2
    block = width // 4
    repeat = (
        lax.broadcasted_iota(jnp.int32, (own, pairs), 0) // 2
        == lax.broadcasted_iota(jnp.int32, (own, pairs), 1)
    ).astype(bf16)
    source = lax.broadcasted_iota(jnp.int32, (width, 512), 0)
    lane = lax.broadcasted_iota(jnp.int32, (width, 512), 1)
    spread = ((lane % 128 < block) & (source == lane // 128 * block + lane % 128)).astype(bf16)
    means = pair_mean(pairs, own, 0)
    square = 0.0
    for g in range(groups):
        wide = y_ref[g, :own, :].astype(f32)
        square = square + jnp.sum(wide * wide, axis=1, keepdims=True)
    inv = lax.rsqrt(square / full + EPSILON)
    slopes, inner = [], 0.0
    for g in range(groups):
        normed = y_ref[g, :own, :].astype(f32) * inv
        half = half_erf(normed)
        features = exact_dot(means, normed * half).astype(bf16)
        placed = jnp.dot(features, spread, preferred_element_type=f32).astype(bf16)
        for i in range(4):
            back_ref[4 * g + i, :pairs, :] = placed[:, 128 * i : 128 * i + 128]
        upstream = 0.5 * jnp.dot(repeat, y_ref[g, own:, :], preferred_element_type=f32)
        slope = upstream * gelu_slope(normed, half)
        inner = inner + jnp.sum(slope * normed, axis=1, keepdims=True)
        slopes.append(slope)
    mean = inner / full
    for g in range(groups):
        normed = y_ref[g, :own, :].astype(f32) * inv
        grad = (inv * (slopes[g] - normed * mean)).astype(bf16)
        grad_ref[g] = grad
        head_ref[g] = grad_ref[g, :8, :]
        tail_ref[g] = grad_ref[g, own - 8 :, :]
        placed = jnp.dot(grad, spread, preferred_element_type=f32).astype(bf16)
        for i in range(4):
            back_ref[4 * g + i, pairs:, :] = placed[:, 128 * i : 128 * i + 128]


def statistics(conv_out, own):
    groups, _, width = conv_out.shape
    shapes = (
        jax.ShapeDtypeStruct((groups, own, width), bf16),
        jax.ShapeDtypeStruct((4 * groups, own + own // 2, 128), bf16),
        jax.ShapeDtypeStruct((groups, 8, width), bf16),
        jax.ShapeDtypeStruct((groups, 8, width), bf16),
    )
    kernel = functools.partial(statistics_kernel, own)
    return local_call(kernel, shapes, [], conv_out)


def input_kernel(act_ref, *refs):
    part_refs, out_ref = refs[:4], refs[4]
    rows = act_ref.shape[0]
    pooled_grad = sum(ref[...].astype(f32) for ref in part_refs)
    pair = lax.broadcasted_iota(jnp.int32, (rows, rows // 2), 1)
    row = lax.broadcasted_iota(jnp.int32, (rows, rows // 2), 0)
    upstream = exact_dot(jnp.where(row // 2 == pair, 0.5, 0.0), pooled_grad)
    wide = act_ref[...].astype(f32)
    inv = lax.rsqrt(jnp.mean(wide * wide, axis=1, keepdims=True) + EPSILON)
    normed = wide * inv
    slope = upstream * gelu_slope(normed, half_erf(normed))
    inner = jnp.mean(slope * normed, axis=1, keepdims=True)
    out_ref[...] = (inv * (slope - normed * inner)).astype(bf16)


def input_gradient(activations, parts):
    shape = jax.ShapeDtypeStruct(activations.shape, bf16)
    return local_call(input_kernel, shape, [], activations, *parts)


def weight_kernel(taps, block, where_ref, back_ref, *refs):
    ring_refs, (mine_ref, other_ref, feature_ref, stage_ref, wide_ref, part_ref) = refs[:4], refs[4:]
    count, rows, lanes = back_ref.shape
    pooled = rows // 3
    own = 2 * pooled
    span = wide_ref.shape[1] // 4
    width = wide_ref.shape[2]
    core, y = where_ref[0], where_ref[2]
    source = lax.broadcasted_iota(jnp.int32, (lanes, width), 0)
    lane = lax.broadcasted_iota(jnp.int32, (lanes, width), 1)
    for b in range(count):
        feature_ref[pl.ds(b * pooled, pooled), :] = back_ref[b, :pooled, :block]
    stage_ref[...] = jnp.zeros_like(stage_ref)
    for i in range(4):
        total = jnp.zeros((4 * span, width), f32)
        for k in range(taps):
            for z in range(4):
                stage_ref[pl.ds(z * span + k + 2, own), :] = back_ref[
                    4 * z + i, pooled:, :
                ].astype(f32)
                stage_ref[pl.ds(z * span + k + 1, 1), :] = jnp.zeros((1, lanes), f32)
            place = ((source < block) & (lane == source + k * block)).astype(bf16)
            total = total + jnp.dot(
                stage_ref[...].astype(bf16), place, preferred_element_type=f32
            )
        for z in range(4):
            stage_ref[pl.ds(z * span + taps + 1, own), :] = jnp.zeros((own, lanes), f32)
        wide_ref[i] = total.astype(bf16)
    contract = (((0,), (0,)), ((), ()))
    for j, turns in enumerate((0, 3, 1, 2)):
        term = lax.dot_general(
            ring_refs[j][...], wide_ref[lax.rem(y + turns, 4)], contract,
            preferred_element_type=f32,
        )
        part_ref[...] = term if j == 0 else part_ref[...] + term
    for c in range(mine_ref.shape[0]):
        step = mine_ref.shape[1]
        near = pl.ds(pl.multiple_of(c * 2 * step + core * step, step), step)
        far = pl.ds(pl.multiple_of(c * 2 * step + (1 - core) * step, step), step)
        at = c % 4 * 4 + c // 4
        mine_ref[at] = part_ref[near, : taps * block]
        other_ref[at] = part_ref[far, : taps * block].astype(bf16)


def weight_partial(where, back, ring, taps, block):
    count, rows, lanes = back.shape
    total, width = ring[0].shape
    lot = (16, width // 32, taps * block)
    wide = (taps * block + 127) // 128 * 128
    shapes = (
        jax.ShapeDtypeStruct(lot, f32),
        jax.ShapeDtypeStruct(lot, bf16),
        jax.ShapeDtypeStruct((count * (rows // 3), block), bf16),
    )
    scratch = [
        pltpu.VMEM((total, lanes), f32),
        pltpu.VMEM((4, total, wide), bf16),
        pltpu.VMEM((width, wide), f32),
    ]
    kernel = functools.partial(weight_kernel, taps, block)
    return local_call(kernel, shapes, scratch, where, back, *ring, limit=16)


def per_device(activations, conv_weight, cotangent):
    tap_count, out_width, in_width = conv_weight.shape
    core = lax.axis_index("core")
    zl, y = lax.axis_index("zl"), lax.axis_index("y")
    half = in_width // 2
    rows = activations.shape[0] // 2
    span = rows + 8
    group = 4 * out_width
    lanes = 4 * span
    step = rows // 2

    low = shift(activations[-8:], AXES, 1)
    high = shift(activations[:8], AXES, -1)

    where = jnp.stack([core, zl, y]).astype(jnp.int32)
    own_cot, *packs = pack_shards(where, conv_weight, cotangent)
    packs = [turn(packs[j], "y", j + 1) for j in range(3)]
    shards = [jnp.where(core == 0, conv_weight[:, :, :half], conv_weight[:, :, half:])]
    shards += [pack[step:].reshape(tap_count, out_width, half) for pack in packs]
    first = jnp.zeros((tap_count, 4, out_width, half), bf16)
    first = lax.dynamic_update_slice_in_dim(first, shards[0][:, None], y, axis=1)
    for j in range(1, 4):
        first = lax.dynamic_update_slice_in_dim(first, shards[j][:, None], (y - j) % 4, axis=1)
    first = first.reshape(tap_count, group, half)
    second = lax.ppermute(first, "core", [(0, 1), (1, 0)])

    block = pooled_block(low, activations, high)
    gathered = gather_all(block, "zl")
    flat = gathered.reshape(lanes, in_width)

    conv_out = conv_forward(where, flat, first, second, own_cot, packs)
    up, down = turn(flat, "y", 1), turn(flat, "y", -1)
    far = turn(flat, "y", 2)
    conv_out = lax.all_to_all(conv_out, "zl", 0, 0)
    grad, back, head, tail = statistics(conv_out, rows)
    back = lax.all_to_all(back, SUB, 0, 0)
    tail, head = shift(tail, AXES, 1), shift(head, AXES, -1)
    framed = jnp.concatenate([tail, grad, head], axis=1)
    framed = lax.all_to_all(framed, "zl", 0, 0)

    own = conv_backward(where, framed.reshape(-1, group), first, second, rows)
    parts = [own[0], turn(own[2], "zl", 2)]
    parts = parts + [turn(own[1], "zl", 1), turn(own[3], "zl", 3)]
    input_grad = input_gradient(activations, parts)

    mine, other, features = weight_partial(
        where, back, [flat, up, down, far], tap_count, out_width
    )
    other = lax.ppermute(other, "core", [(0, 1), (1, 0)])
    total = (mine + other.astype(f32)).astype(bf16)
    total = lax.all_to_all(total.reshape(4, 4, *total.shape[1:]), "x", 0, 0)
    total = jnp.sum(total.astype(f32), axis=0).astype(bf16)
    total = lax.all_to_all(total, "zh", 0, 0)
    weight_grad = jnp.sum(total.astype(f32), axis=0).reshape(-1, tap_count, out_width)
    return (features, input_grad, weight_grad)


def solution(mesh):
    split = Mesh(mesh.devices.reshape(4, 4, 2, 4, 4), AXES)
    return jax.shard_map(
        per_device,
        mesh=split,
        in_specs=(P(AXES, None), P(None, SUB, None), P(SEQ, SUB)),
        out_specs=(P(SEQ, SUB), P(AXES, None), P(SEQ, None, SUB)),
        check_vma=False,
    )
```

```python
import functools

import jax
import jax.numpy as jnp
from jax import lax
from jax.experimental import pallas as pl
from jax.experimental.pallas import tpu as pltpu
from jax.sharding import Mesh, PartitionSpec as P


EPSILON = 1e-06
AXES = ("zh", "x", "core", "zl", "y")
SEQ = ("zh", "x", "core")
SUB = ("zl", "y")
bf16 = jnp.bfloat16
f32 = jnp.float32


def half_erf(tensor):
    return 0.5 * (1.0 + lax.erf(tensor * 0.7071067811865476))


def gelu_slope(tensor, half):
    return half + tensor * jnp.exp(-0.5 * tensor * tensor) * 0.3989422804014327


def shift(block, axis, step):
    count = lax.axis_size(axis)
    pairs = [(i, i + step) for i in range(count) if 0 <= i + step < count]
    return lax.ppermute(block, axis, pairs)


def turn(block, axis, step):
    count = lax.axis_size(axis)
    return lax.ppermute(block, axis, [(i, (i + step) % count) for i in range(count)])


def gather_all(block, axis):
    count = lax.axis_size(axis)
    return lax.all_to_all(jnp.broadcast_to(block, (count, *block.shape)), axis, 0, 0)


def local_call(kernel, shapes, scratch, *args, limit=12):
    vmem = pl.BlockSpec(memory_space=pltpu.VMEM)
    return pl.pallas_call(
        kernel,
        out_shape=shapes,
        in_specs=[
            pl.BlockSpec(memory_space=pltpu.SMEM) if a.dtype == jnp.int32 else vmem for a in args
        ],
        out_specs=jax.tree.map(lambda _: vmem, shapes),
        scratch_shapes=scratch,
        compiler_params=pltpu.CompilerParams(vmem_limit_bytes=limit << 20),
    )(*args)


def exact_dot(left, right):
    return jnp.dot(left, right, precision=lax.Precision.HIGHEST, preferred_element_type=f32)


def pair_mean(count, rows, first):
    pair = lax.broadcasted_iota(jnp.int32, (count, rows), 0)
    row = lax.broadcasted_iota(jnp.int32, (count, rows), 1)
    return jnp.where((row - first >= 2 * pair) & (row - first <= 2 * pair + 1), 0.5, 0.0)


def pooled_kernel(low_ref, own_ref, high_ref, out_ref, gelu_ref):
    at = 0
    for ref in (low_ref, own_ref, high_ref):
        count = ref.shape[0]
        wide = ref[...].astype(f32)
        inv = lax.rsqrt(jnp.mean(wide * wide, axis=1, keepdims=True) + EPSILON)
        normed = wide * inv
        gelu_ref[at : at + count, :] = normed * half_erf(normed)
        at += count
    out_ref[...] = exact_dot(pair_mean(at // 2, at, 0), gelu_ref[...]).astype(bf16)


def pooled_block(low, own, high):
    total = low.shape[0] + own.shape[0] + high.shape[0]
    width = own.shape[1]
    return local_call(
        pooled_kernel, jax.ShapeDtypeStruct((total // 2, width), bf16),
        [pltpu.VMEM((total, width), f32)], low, own, high,
    )


def conv_kernel(where_ref, flat_ref, first_ref, second_ref, *refs):
    cot_refs, out_ref, tap_ref = refs[:4], refs[4], refs[5]
    lanes = flat_ref.shape[0]
    taps, group, half = first_ref.shape
    core, y = where_ref[0], where_ref[2]
    span = lanes // 4
    own = span - 8
    step, block = cot_refs[0].shape[1:]
    near = flat_ref[:, pl.ds(pl.multiple_of(core * half, 128), half)]
    far = flat_ref[:, pl.ds(pl.multiple_of((1 - core) * half, 128), half)]
    contract = (((1,), (1,)), ((), ()))
    for k in range(taps):
        tap_ref[k, lanes:, :] = jnp.zeros_like(tap_ref[k, lanes:, :])
        tap_ref[k, :lanes, :] = lax.dot_general(
            near, first_ref[k], contract, preferred_element_type=f32
        ) + lax.dot_general(far, second_ref[k], contract, preferred_element_type=f32)
    source = lax.broadcasted_iota(jnp.int32, (block, group), 0)
    lane = lax.broadcasted_iota(jnp.int32, (block, group), 1)
    for f in range(4):
        total = tap_ref[0, pl.ds(f * span + 2, own), :]
        for k in range(1, taps):
            total = total + tap_ref[k, pl.ds(f * span + 2 + k, own), :]
        out_ref[f, :own, :] = total.astype(bf16)
        placed = jnp.zeros((step, group), f32)
        for j in range(4):
            place = (lane == source + lax.rem(y - j + 4, 4) * block).astype(bf16)
            placed = placed + jnp.dot(cot_refs[j][f], place, preferred_element_type=f32)
        out_ref[f, own:, :] = placed.astype(bf16)


def conv_forward(where, flat, first, second, cots):
    taps, group, _ = first.shape
    span = flat.shape[0] // 4
    shape = jax.ShapeDtypeStruct((4, span - 8 + cots[0].shape[1], group), bf16)
    scratch = [pltpu.VMEM((taps, flat.shape[0] + 8, group), f32)]
    return local_call(conv_kernel, shape, scratch, where, flat, first, second, *cots)


def backward_kernel(rows, where_ref, flat_ref, first_ref, second_ref, *refs):
    out_refs, tap_ref = refs[:4], refs[4]
    taps, _, half = first_ref.shape
    frame = flat_ref.shape[0] // 4
    core, zl = where_ref[0], where_ref[1]
    for side, weight_ref in ((core, first_ref), (1 - core, second_ref)):
        for k in range(taps):
            spread = jnp.dot(flat_ref[...], weight_ref[k], preferred_element_type=f32)
            for f in range(4):
                tap_ref[k, f] = spread[f * frame : (f + 1) * frame]
        for j in range(4):
            f = lax.rem(zl + j, 4)
            total = tap_ref[0, f, pl.ds(10, rows), :]
            for k in range(1, taps):
                total = total + tap_ref[k, f, pl.ds(10 - k, rows), :]
            columns = pl.ds(pl.multiple_of(side * half, 128), half)
            out_refs[j][:, columns] = total.astype(bf16)


def conv_backward(where, flat, first, second, rows):
    taps, _, half = first.shape
    shapes = (jax.ShapeDtypeStruct((rows, 2 * half), bf16),) * 4
    scratch = [pltpu.VMEM((taps, 4, flat.shape[0] // 4, half), f32)]
    kernel = functools.partial(backward_kernel, rows)
    return local_call(kernel, shapes, scratch, where, flat, first, second, limit=16)


def statistics_kernel(own, y_ref, grad_ref, back_ref, head_ref, tail_ref):
    groups, _, width = y_ref.shape
    full = groups * width
    pairs = own // 2
    block = width // 4
    repeat = (
        lax.broadcasted_iota(jnp.int32, (own, pairs), 0) // 2
        == lax.broadcasted_iota(jnp.int32, (own, pairs), 1)
    ).astype(bf16)
    source = lax.broadcasted_iota(jnp.int32, (width, 512), 0)
    lane = lax.broadcasted_iota(jnp.int32, (width, 512), 1)
    spread = ((lane % 128 < block) & (source == lane // 128 * block + lane % 128)).astype(bf16)
    means = pair_mean(pairs, own, 0)
    square = 0.0
    for g in range(groups):
        wide = y_ref[g, :own, :].astype(f32)
        square = square + jnp.sum(wide * wide, axis=1, keepdims=True)
    inv = lax.rsqrt(square / full + EPSILON)
    slopes, inner = [], 0.0
    for g in range(groups):
        normed = y_ref[g, :own, :].astype(f32) * inv
        half = half_erf(normed)
        features = exact_dot(means, normed * half).astype(bf16)
        placed = jnp.dot(features, spread, preferred_element_type=f32).astype(bf16)
        for i in range(4):
            back_ref[4 * g + i, :pairs, :] = placed[:, 128 * i : 128 * i + 128]
        upstream = 0.5 * jnp.dot(repeat, y_ref[g, own:, :], preferred_element_type=f32)
        slope = upstream * gelu_slope(normed, half)
        inner = inner + jnp.sum(slope * normed, axis=1, keepdims=True)
        slopes.append(slope)
    mean = inner / full
    for g in range(groups):
        normed = y_ref[g, :own, :].astype(f32) * inv
        grad = (inv * (slopes[g] - normed * mean)).astype(bf16)
        grad_ref[g] = grad
        head_ref[g] = grad_ref[g, :8, :]
        tail_ref[g] = grad_ref[g, own - 8 :, :]
        placed = jnp.dot(grad, spread, preferred_element_type=f32).astype(bf16)
        for i in range(4):
            back_ref[4 * g + i, pairs:, :] = placed[:, 128 * i : 128 * i + 128]


def statistics(conv_out, own):
    groups, _, width = conv_out.shape
    shapes = (
        jax.ShapeDtypeStruct((groups, own, width), bf16),
        jax.ShapeDtypeStruct((4 * groups, own + own // 2, 128), bf16),
        jax.ShapeDtypeStruct((groups, 8, width), bf16),
        jax.ShapeDtypeStruct((groups, 8, width), bf16),
    )
    kernel = functools.partial(statistics_kernel, own)
    return local_call(kernel, shapes, [], conv_out)


def input_kernel(act_ref, *refs):
    part_refs, out_ref = refs[:4], refs[4]
    rows = act_ref.shape[0]
    pooled_grad = sum(ref[...].astype(f32) for ref in part_refs)
    pair = lax.broadcasted_iota(jnp.int32, (rows, rows // 2), 1)
    row = lax.broadcasted_iota(jnp.int32, (rows, rows // 2), 0)
    upstream = exact_dot(jnp.where(row // 2 == pair, 0.5, 0.0), pooled_grad)
    wide = act_ref[...].astype(f32)
    inv = lax.rsqrt(jnp.mean(wide * wide, axis=1, keepdims=True) + EPSILON)
    normed = wide * inv
    slope = upstream * gelu_slope(normed, half_erf(normed))
    inner = jnp.mean(slope * normed, axis=1, keepdims=True)
    out_ref[...] = (inv * (slope - normed * inner)).astype(bf16)


def input_gradient(activations, parts):
    shape = jax.ShapeDtypeStruct(activations.shape, bf16)
    return local_call(input_kernel, shape, [], activations, *parts)


def weight_kernel(taps, block, where_ref, back_ref, *refs):
    ring_refs, (mine_ref, other_ref, feature_ref, stage_ref, wide_ref, part_ref) = refs[:4], refs[4:]
    count, rows, lanes = back_ref.shape
    pooled = rows // 3
    own = 2 * pooled
    span = wide_ref.shape[1] // 4
    width = wide_ref.shape[2]
    core, y = where_ref[0], where_ref[2]
    source = lax.broadcasted_iota(jnp.int32, (lanes, width), 0)
    lane = lax.broadcasted_iota(jnp.int32, (lanes, width), 1)
    for b in range(count):
        feature_ref[pl.ds(b * pooled, pooled), :] = back_ref[b, :pooled, :block]
    stage_ref[...] = jnp.zeros_like(stage_ref)
    for i in range(4):
        total = jnp.zeros((4 * span, width), f32)
        for k in range(taps):
            for z in range(4):
                stage_ref[pl.ds(z * span + k + 2, own), :] = back_ref[
                    4 * z + i, pooled:, :
                ].astype(f32)
                stage_ref[pl.ds(z * span + k + 1, 1), :] = jnp.zeros((1, lanes), f32)
            place = ((source < block) & (lane == source + k * block)).astype(bf16)
            total = total + jnp.dot(
                stage_ref[...].astype(bf16), place, preferred_element_type=f32
            )
        for z in range(4):
            stage_ref[pl.ds(z * span + taps + 1, own), :] = jnp.zeros((own, lanes), f32)
        wide_ref[i] = total.astype(bf16)
    contract = (((0,), (0,)), ((), ()))
    for j, turns in enumerate((0, 3, 1, 2)):
        term = lax.dot_general(
            ring_refs[j][...], wide_ref[lax.rem(y + turns, 4)], contract,
            preferred_element_type=f32,
        )
        part_ref[...] = term if j == 0 else part_ref[...] + term
    for c in range(mine_ref.shape[0]):
        step = mine_ref.shape[1]
        near = pl.ds(pl.multiple_of(c * 2 * step + core * step, step), step)
        far = pl.ds(pl.multiple_of(c * 2 * step + (1 - core) * step, step), step)
        at = c % 4 * 4 + c // 4
        mine_ref[at] = part_ref[near, : taps * block]
        other_ref[at] = part_ref[far, : taps * block].astype(bf16)


def weight_partial(where, back, ring, taps, block):
    count, rows, lanes = back.shape
    total, width = ring[0].shape
    lot = (16, width // 32, taps * block)
    wide = (taps * block + 127) // 128 * 128
    shapes = (
        jax.ShapeDtypeStruct(lot, f32),
        jax.ShapeDtypeStruct(lot, bf16),
        jax.ShapeDtypeStruct((count * (rows // 3), block), bf16),
    )
    scratch = [
        pltpu.VMEM((total, lanes), f32),
        pltpu.VMEM((4, total, wide), bf16),
        pltpu.VMEM((width, wide), f32),
    ]
    kernel = functools.partial(weight_kernel, taps, block)
    return local_call(kernel, shapes, scratch, where, back, *ring, limit=16)


def per_device(activations, conv_weight, cotangent):
    tap_count, out_width, in_width = conv_weight.shape
    core = lax.axis_index("core")
    zl, y = lax.axis_index("zl"), lax.axis_index("y")
    half = in_width // 2
    rows = activations.shape[0] // 2
    span = rows + 8
    group = 4 * out_width
    lanes = 4 * span
    step = rows // 2

    low = shift(activations[-8:], AXES, 1)
    high = shift(activations[:8], AXES, -1)

    own_half = jnp.where(core == 0, conv_weight[:, :, :half], conv_weight[:, :, half:])
    own_half = lax.optimization_barrier(own_half)
    shards = [own_half] + [turn(own_half, "y", j) for j in (1, 2, 3)]
    first = jnp.zeros((tap_count, 4, out_width, half), bf16)
    first = lax.dynamic_update_slice_in_dim(first, shards[0][:, None], y, axis=1)
    for j in range(1, 4):
        first = lax.dynamic_update_slice_in_dim(first, shards[j][:, None], (y - j) % 4, axis=1)
    first = first.reshape(tap_count, group, half)
    second = lax.ppermute(first, "core", [(0, 1), (1, 0)])

    block = pooled_block(low, activations, high)
    gathered = gather_all(block, "zl")
    flat = gathered.reshape(lanes, in_width)
    where = jnp.stack([core, zl, y]).astype(jnp.int32)

    cot, _ = lax.optimization_barrier((cotangent, block))
    cot = cot.reshape(4, 4, step, out_width)
    cots = [lax.dynamic_index_in_dim(cot, (y + j) % 4, 1, keepdims=False) for j in range(4)]
    second_cot = turn(cots[2], "y", 2)
    first_cot = turn(cots[1], "y", 1)
    cots = [cots[0], first_cot, second_cot, turn(cots[3], "y", 3)]

    conv_out = conv_forward(where, flat, first, second, cots)
    up, down = turn(flat, "y", 1), turn(flat, "y", -1)
    far = turn(flat, "y", 2)
    conv_out = lax.all_to_all(conv_out, "zl", 0, 0)
    grad, back, head, tail = statistics(conv_out, rows)
    back = lax.all_to_all(back, SUB, 0, 0)
    tail, head = shift(tail, AXES, 1), shift(head, AXES, -1)
    framed = jnp.concatenate([tail, grad, head], axis=1)
    framed = lax.all_to_all(framed, "zl", 0, 0)

    own = conv_backward(where, framed.reshape(-1, group), first, second, rows)
    parts = [own[0], turn(own[2], "zl", 2), turn(own[1], "zl", 1)]
    parts = parts + [turn(own[3], "zl", 3)]
    input_grad = input_gradient(activations, parts)

    mine, other, features = weight_partial(
        where, back, [flat, up, down, far], tap_count, out_width
    )
    other = lax.ppermute(other, "core", [(0, 1), (1, 0)])
    total = (mine + other.astype(f32)).astype(bf16)
    total = lax.all_to_all(total.reshape(4, 4, *total.shape[1:]), "x", 0, 0)
    total = jnp.sum(total.astype(f32), axis=0).astype(bf16)
    total = lax.all_to_all(total, "zh", 0, 0)
    weight_grad = jnp.sum(total.astype(f32), axis=0).reshape(-1, tap_count, out_width)
    return (features, input_grad, weight_grad)


def solution(mesh):
    split = Mesh(mesh.devices.reshape(4, 4, 2, 4, 4), AXES)
    return jax.shard_map(
        per_device,
        mesh=split,
        in_specs=(P(AXES, None), P(None, SUB, None), P(SEQ, SUB)),
        out_specs=(P(SEQ, SUB), P(AXES, None), P(SEQ, None, SUB)),
        check_vma=False,
    )
```
